768 devices in a mesh: axial: 96 (over x, z, y_lo), azim: 8 (over y_hi, core).
Axes of the slice: x: 4, y: 8 (y_hi: 4, y_lo: 2; y = y_hi * 2 + y_lo), z: 12, core: 2. Of those that a mesh axis runs over, the one named last changes fastest.
Arguments:
- source: float32 [12, 384, 128, 256], P(None, 'axial', 'azim'), may hold values from -24 to 24
- storage: float32 [12, 384, 128, 256], P(None, 'axial', 'azim'), may hold values from 0.5 to 2
- materials: int32 [384, 128, 256], P('axial', 'azim'), may hold values from 0 to 3
- conductance: float32 [12], replicated, may hold values from 0.3 to 2
- mixing: float32 [4, 12, 12], replicated, may hold values from -0.9 to 0.9
- counts: int32 [96, 8], P('axial', 'azim'), may hold values from 30 to 120, as said below
- vis_owner: int32 [96, 8, 120, 4], P('axial', 'azim'), may hold values from 0 to 95, as said below
- vis_slot: int32 [96, 8, 120, 4], P('axial', 'azim'), may hold values from 0 to 119, as said below
- vis_block: int32 [96, 8, 120, 4], P('axial', 'azim'), may hold values from 0 to 7
- radiosity_old: bfloat16 [96, 8, 120, 128], P('axial', 'azim'), may hold values from -6 to 6
- view_blocks: bfloat16 [8, 128, 128], replicated, may hold values from -0.25 to 0.25
- emission: float32 [96, 8, 120, 128], P('axial', 'azim'), may hold values from 0.5 to 1.5
- reflect: float32 [96, 8, 120, 128], P('axial', 'azim'), may hold values from 0.2 to 0.8
Outputs:
- solution: float32 [12, 384, 128, 256], P(None, 'axial', 'azim')
- residual: float32 [12, 384, 128, 256], P(None, 'axial', 'azim')
- radiosity_new: float32 [96, 8, 120, 128], P('axial', 'azim')
The draws below stay inside these ranges and needn't reach their ends.
Inputs may be any that keep to these rules, and one draw needn't show every extreme that they name: Slots 0 to counts - 1 of a device hold its panels; some device has exactly 120. `vis_owner`: owners lie in the same azimuthal column as the panel. Among the entries of the live panels of one device, no owner is named more than 5 times; some device names every owner exactly 5 times, and some owner is named exactly 5 times by every device. `vis_slot`: every entry is below the count of the named owner in the same azimuthal column.
All inputs are finite; a program needn't handle non-finite values.
Results may differ from the reference program's by a relative error of at most 0.0004.
Values may be sent and summed in bfloat16 or wider, within the bound.
A program may use at most 128 MiB of HBM per device.

```python
import math
import jax
import jax.numpy as jnp
from jax import lax

NF = 12
MATS = 4
VIS = 4
NB = 8
ITERS = 3
CA = 4
CZ = 16
CR = 256
PSLOT = 120
RAD = 128
NA = 384
NZ = 128
CAP = 5
N_AXIAL = 96
N_AZIM = 8


def visibility(base_key):
    seed_key = jax.random.fold_in(base_key, 4242)
    count_key, full_key, owner_key, slot_key, star_key = jax.random.split(seed_key, 5)
    total = VIS * PSLOT
    lowest = PSLOT // 4
    devices = N_AXIAL * N_AZIM
    levels = jax.random.randint(count_key, (devices,), 0, 1000)
    counts_flat = lowest + (PSLOT - lowest) * levels * levels // 1000000
    fullest = jax.random.randint(full_key, (), 0, devices)
    counts_flat = jnp.where(jnp.arange(devices) == fullest, PSLOT, counts_flat).astype(jnp.int32)
    counts = counts_flat.reshape(N_AXIAL, N_AZIM)
    starred = jax.random.randint(star_key, (), 0, N_AXIAL)
    base_owner = (jnp.arange(total) // CAP).astype(jnp.int32)

    def one_device(device_key, live_count):
        first_key, second_key = jax.random.split(device_key)
        order_one = jax.random.permutation(first_key, total)
        pool = base_owner[jnp.argsort(jnp.where(base_owner == starred, order_one - total, order_one))]
        order_two = jax.random.permutation(second_key, total)
        scores = jnp.where(jnp.arange(total) < VIS * live_count, order_two, order_two + total)
        places = jnp.argsort(scores)
        return jnp.zeros((total,), jnp.int32).at[places].set(pool)
    device_keys = jax.random.split(owner_key, devices)
    owners = jax.vmap(one_device)(device_keys, counts_flat).reshape(N_AXIAL, N_AZIM, PSLOT, VIS)
    column = jnp.arange(N_AZIM)[None, :, None, None]
    limits = counts[owners, column]
    slots = jax.random.randint(slot_key, owners.shape, 0, limits).astype(jnp.int32)
    return (counts, owners, slots)


def draw_counts(key, part):
    return visibility(key)[0]


def draw_vis_owner(key, part):
    return visibility(key)[1]


def draw_vis_slot(key, part):
    return visibility(key)[2]


def plant(values, rng, smallest, largest):
    shape = values.shape
    place = [jax.random.randint(jax.random.fold_in(rng, axis), (), 0, shape[axis]) for axis in range(len(shape))]
    values = values.at[tuple(place)].set(smallest)
    longest = shape.index(max(shape))
    place[longest] = (place[longest] + 1) % shape[longest]
    return values.at[tuple(place)].set(largest)


def shard_levels(key, dims, cuts, smallest, largest):
    loudness = 1.0
    for position, blocks in cuts:
        draws = jax.random.uniform(jax.random.fold_in(jax.random.fold_in(key, 6), position), (blocks,), jnp.float32, smallest / len(cuts), largest / len(cuts))
        loudness = loudness * jnp.repeat(jnp.exp(draws), dims[position] // blocks).reshape((-1,) + (1,) * (len(dims) - 1 - position))
    return loudness


def noise(own_key, extent, width, reach, cuts=(), held_as=jnp.bfloat16):
    factor_of = shard_levels(own_key, extent, cuts, -0.22, 0.18) if cuts else 1.0
    drawn = jax.random.normal(own_key, extent, jnp.float32) * width * factor_of
    return jnp.minimum(jnp.maximum(drawn, -reach), reach).astype(held_as)


def setup_inputs(seed: int = 0) -> dict:
    streams_of = jax.random.split(jax.random.key(seed), 14)
    return {
        "source": noise(streams_of[0], (NF, NA, NZ, CR), 4.0, 24.0, ((1, 96), (2, 8)), jnp.float32),
        "storage": jnp.clip(jnp.exp(math.log(2.0) - 1.3862944 * jax.random.uniform(streams_of[1], (NF, NA, NZ, CR), jnp.float32) ** shard_levels(streams_of[1], (NF, NA, NZ, CR), ((1, 96), (2, 8)), -0.2, 0.2)), 0.5, 2.0),
        "materials": plant(jax.random.randint(streams_of[2], (NA, NZ, CR), 0, MATS), jax.random.fold_in(streams_of[2], 1), 0, MATS - 1).astype(jnp.int32),
        "conductance": jnp.clip(jnp.exp(jax.random.uniform(streams_of[3], (NF,), jnp.float32, math.log(0.3), math.log(2.0))), 0.3, 2.0),
        "mixing": noise(streams_of[4], (MATS, NF, NF), 0.15, 0.9, (), jnp.float32),
        "counts": draw_counts(jax.random.fold_in(streams_of[13], 71), 0),
        "vis_owner": draw_vis_owner(jax.random.fold_in(streams_of[13], 71), 0),
        "vis_slot": draw_vis_slot(jax.random.fold_in(streams_of[13], 71), 0),
        "vis_block": plant(jax.random.randint(streams_of[8], (N_AXIAL, N_AZIM, PSLOT, VIS), 0, NB), jax.random.fold_in(streams_of[8], 1), 0, NB - 1).astype(jnp.int32),
        "radiosity_old": noise(streams_of[9], (N_AXIAL, N_AZIM, PSLOT, RAD), 1.0, 6.0, ((0, 96), (1, 8))),
        "view_blocks": noise(streams_of[10], (NB, RAD, RAD), (RAD * VIS) ** -0.5, 0.25),
        "emission": jnp.clip(0.5 + 1.0 * jax.random.uniform(streams_of[11], (N_AXIAL, N_AZIM, PSLOT, RAD), jnp.float32) ** shard_levels(streams_of[11], (N_AXIAL, N_AZIM, PSLOT, RAD), ((0, 96), (1, 8)), -0.2, 0.2), 0.5, 1.5),
        "reflect": jnp.clip(0.2 + 0.6 * jax.random.uniform(streams_of[12], (N_AXIAL, N_AZIM, PSLOT, RAD), jnp.float32) ** shard_levels(streams_of[12], (N_AXIAL, N_AZIM, PSLOT, RAD), ((0, 96), (1, 8)), -0.2, 0.2), 0.2, 0.8),
    }


center_value = 14.2
half_width = 13.8


def operate(field, storage, materials, conductance, mixing):
    axial_pad = jnp.pad(field, ((0, 0), (1, 1), (0, 0), (0, 0)))
    radial_pad = jnp.pad(field, ((0, 0), (0, 0), (0, 0), (1, 1)))
    beside = axial_pad[:, 2:] + axial_pad[:, :-2]
    beside = beside + jnp.roll(field, 1, axis=2) + jnp.roll(field, -1, axis=2)
    beside = beside + radial_pad[..., 2:] + radial_pad[..., :-2]
    mixed = jnp.zeros_like(field)
    for material in range(MATS):
        chosen = (materials == material).astype(jnp.float32)
        mixed = mixed + chosen[None] * jnp.einsum("fg,gazr->fazr", mixing[material], field, precision=lax.Precision.HIGHEST)
    return storage * field + mixed + conductance[:, None, None, None] * (6.0 * field - beside)


def reference(source, storage, materials, conductance, mixing, counts, vis_owner, vis_slot, vis_block, radiosity_old, view_blocks, emission, reflect):
    spread_ratio = center_value / half_width
    ratio_now = 1.0 / spread_ratio
    solution = jnp.zeros_like(source)
    residual = source
    direction = source / center_value
    for iteration in range(ITERS):
        solution = solution + direction
        residual = residual - operate(direction, storage, materials, conductance, mixing)
        ratio_next = 1.0 / (2.0 * spread_ratio - ratio_now)
        direction = (ratio_next * ratio_now) * direction + (2.0 * ratio_next / half_width) * residual
        ratio_now = ratio_next
    column = jnp.arange(N_AZIM, dtype=jnp.int32)[None, :, None, None]
    gathered = radiosity_old[vis_owner, column, vis_slot].astype(jnp.float32)
    live = jnp.arange(PSLOT, dtype=jnp.int32)[None, None, :] < counts[:, :, None]
    block_hot = ((vis_block[..., None] == jnp.arange(NB, dtype=jnp.int32)) & live[..., None, None]).astype(jnp.float32)
    grouped = jnp.einsum("azpkb,azpkr->azbpr", block_hot, gathered, precision=lax.Precision.HIGHEST)
    incoming = jnp.einsum("bij,azbpj->azpi", view_blocks.astype(jnp.float32), grouped, precision=lax.Precision.HIGHEST)
    wall = solution[0, :, :, CR - 1].reshape(N_AXIAL, CA, N_AZIM, CZ).transpose(0, 2, 1, 3).reshape(N_AXIAL, N_AZIM, CA * CZ)
    wall_temp = wall[:, :, jnp.arange(PSLOT, dtype=jnp.int32) % (CA * CZ)]
    radiosity_new = jnp.where(live[..., None], emission * wall_temp[..., None] + reflect * incoming, 0.0)
    return (solution, residual, radiosity_new)
```

```python
import functools

import jax
import jax.numpy as jnp
from jax import lax
from jax.experimental import pallas as pl
from jax.experimental.pallas import tpu as pltpu
from jax.sharding import PartitionSpec as P

NF = 12
MATS = 4
VIS = 4
NB = 8
ITERS = 3
CA = 4
CZ = 16
CR = 256
PSLOT = 120
RAD = 128
N_AXIAL = 96
N_AZIM = 8
XN = 4
ZN = 12
YN = 2
XY = XN * YN
CAP = 5
ROWS = 8

center_value = 14.2
half_width = 13.8
MESH = pl.DeviceIdType.MESH


def steps():
    spread = center_value / half_width
    ratio = 1.0 / spread
    out = []
    for _ in range(ITERS - 1):
        after = 1.0 / (2.0 * spread - ratio)
        out.append((after * ratio, 2.0 * after / half_width))
        ratio = after
    return out


def kernel(
    source, storage, materials, cond, mixing, counts, owner, slot, block, rad, view,
    emission, reflect,
    x_out, r_out, rad_out,
    dirs, coef, stor, mats, halo_a, halo_z, pack_z,
    ask, ask_a, ask_b, rows_out, rows_a, rows_b, radp, idx, tcol,
    load_sem, sa_send, sa_recv, sz_send, sz_recv,
    qa_send, qa_recv, qb_send, qb_recv, pa_send, pa_recv, pb_send, pb_recv,
):
    ax = lax.axis_index("axial")
    az = lax.axis_index("azim")
    y_pos = ax % YN
    xz = ax // YN
    z_pos = xz % ZN
    x_pos = xz // ZN
    xy_pos = x_pos * YN + y_pos

    def z_peer(k):
        z = (z_pos + k) % ZN
        return z, (x_pos * ZN + z) * YN + y_pos

    def xy_peer(k):
        q = (xy_pos + k) % XY
        return q, ((q // YN) * ZN + z_pos) * YN + q % YN

    before = (ax + N_AXIAL - 1) % N_AXIAL
    after = (ax + 1) % N_AXIAL
    left = (az + N_AZIM - 1) % N_AZIM
    right = (az + 1) % N_AZIM

    loads = [
        pltpu.make_async_copy(source, r_out, load_sem.at[0]),
        pltpu.make_async_copy(materials, mats, load_sem.at[1]),
        pltpu.make_async_copy(storage, stor, load_sem.at[2]),
    ]
    for copy in loads:
        copy.start()

    barrier = pltpu.get_barrier_semaphore()
    for dev in (before, after):
        pl.semaphore_signal(barrier, inc=1, device_id={"axial": dev}, device_id_type=MESH)
    for dev in (left, right):
        pl.semaphore_signal(barrier, inc=1, device_id={"azim": dev}, device_id_type=MESH)
    for k in range(1, ZN):
        pl.semaphore_signal(barrier, inc=1, device_id={"axial": z_peer(k)[1]}, device_id_type=MESH)
    for k in range(1, XY):
        pl.semaphore_signal(barrier, inc=1, device_id={"axial": xy_peer(k)[1]}, device_id_type=MESH)

    def zero_rims(a, carry):
        for it in range(ITERS):
            for f in range(NF):
                dirs[it, f, a, 0:8, :] = jnp.zeros((8, CR), jnp.float32)
                dirs[it, f, a, 24:32, :] = jnp.zeros((8, CR), jnp.float32)
        return carry

    lax.fori_loop(1, CA + 1, zero_rims, 0)
    for it in range(ITERS):
        for f in range(NF):
            dirs[it, f, 0, 8:24, :] = jnp.zeros((CZ, CR), jnp.float32)
            dirs[it, f, CA + 1, 8:24, :] = jnp.zeros((CZ, CR), jnp.float32)

    pl.semaphore_wait(barrier, 4 + (ZN - 1) + (XY - 1))

    def send_axial(it, low, high):
        one = pltpu.make_async_remote_copy(
            low, halo_a.at[it, 1], sa_send.at[it, 0], sa_recv.at[it, 1],
            device_id={"axial": before}, device_id_type=MESH)
        two = pltpu.make_async_remote_copy(
            high, halo_a.at[it, 0], sa_send.at[it, 1], sa_recv.at[it, 0],
            device_id={"axial": after}, device_id_type=MESH)
        one.start()
        two.start()
        return [one, two]

    def send_azim(it):
        one = pltpu.make_async_remote_copy(
            pack_z.at[it, 0], halo_z.at[it, 1], sz_send.at[it, 0], sz_recv.at[it, 1],
            device_id={"azim": left}, device_id_type=MESH)
        two = pltpu.make_async_remote_copy(
            pack_z.at[it, 1], halo_z.at[it, 0], sz_send.at[it, 1], sz_recv.at[it, 0],
            device_id={"azim": right}, device_id_type=MESH)
        one.start()
        two.start()
        return [one, two]

    sent = send_axial(0, source.at[:, 0], source.at[:, CA - 1])
    loads[0].wait()
    for f in range(NF):
        for a in range(CA):
            value = r_out[f, a] * (1.0 / center_value)
            dirs[0, f, a + 1, 8:24, :] = value
            pack_z[0, 0, f, a] = value[0:1, :]
            pack_z[0, 1, f, a] = value[CZ - 1 : CZ, :]
    halos = [sent + send_azim(0)]

    live_count = counts[0, 0]
    lane = lax.broadcasted_iota(jnp.int32, (1, RAD), 1)
    live = lane < live_count
    idx[...] = jnp.zeros((24, RAD), jnp.int32)
    idx[0:VIS, 0:PSLOT] = owner[...]
    idx[8 : 8 + VIS, 0:PSLOT] = slot[...]
    idx[16 : 16 + VIS, 0:PSLOT] = block[...]
    sub96 = lax.broadcasted_iota(jnp.int32, (N_AXIAL, RAD), 0)
    lane96 = lax.broadcasted_iota(jnp.int32, (N_AXIAL, RAD), 1)
    upper = (
        lax.broadcasted_iota(jnp.int32, (RAD, RAD), 0)
        < lax.broadcasted_iota(jnp.int32, (RAD, RAD), 1)
    ).astype(jnp.float32).astype(jnp.bfloat16)
    ones = jnp.ones((RAD, RAD), jnp.bfloat16)
    past = jnp.zeros((N_AXIAL, RAD), jnp.float32)
    hits, ranks = [], []
    tcol[...] = jnp.zeros((RAD, RAD), jnp.float32)
    for k in range(VIS):
        own = idx[k : k + 1, :]
        y_of = own % YN
        t = own // YN
        x_of = (
            (t >= ZN).astype(jnp.int32)
            + (t >= 2 * ZN).astype(jnp.int32)
            + (t >= 3 * ZN).astype(jnp.int32)
        )
        place = (t - ZN * x_of) * XY + x_of * YN + y_of
        place = jnp.where(live, place, -1)
        hit = (sub96 == place).astype(jnp.float32)
        hit_b = hit.astype(jnp.bfloat16)
        rank = jnp.dot(hit_b, upper, preferred_element_type=jnp.float32)
        if k > 0:
            rank = rank + jnp.dot(
                past.astype(jnp.bfloat16), ones, preferred_element_type=jnp.float32)
        past = past + hit
        hits.append(hit)
        ranks.append(rank)
        mine = jnp.sum(hit * rank, axis=0, keepdims=True)
        tcol[k : k + 1, :] = place.astype(jnp.float32) * ROWS + mine
        tcol[8 + k : 9 + k, :] = idx[16 + k : 17 + k, :].astype(jnp.float32)
    asked = jnp.full((N_AXIAL, RAD), -1, jnp.int32)
    for r in range(CAP):
        total = jnp.zeros((N_AXIAL, RAD), jnp.float32)
        for k in range(VIS):
            wanted = (idx[8 + k : 9 + k, :] + 1).astype(jnp.float32)
            total = total + jnp.where(ranks[k] == float(r), hits[k] * wanted, 0.0)
        value = jnp.sum(total, axis=1, keepdims=True).astype(jnp.int32) - 1
        asked = jnp.where(lane96 == r, value, asked)
    ask[...] = asked.reshape(ZN, XY, 1, RAD)
    ask_a[z_pos] = ask[z_pos]
    q_a = []
    for k in range(1, ZN):
        z, dev = z_peer(k)
        copy = pltpu.make_async_remote_copy(
            ask.at[z], ask_a.at[z_pos], qa_send.at[k], qa_recv.at[k],
            device_id={"axial": dev}, device_id_type=MESH)
        copy.start()
        q_a.append(copy)

    for copy in loads[1:]:
        copy.wait()

    def build(a, carry):
        kind = mats[a]
        odd = (kind % 2) == 1
        high = kind >= 2
        for f in range(NF):
            for g in range(NF):
                low_c = jnp.where(odd, mixing[1, f, g], mixing[0, f, g])
                high_c = jnp.where(odd, mixing[3, f, g], mixing[2, f, g])
                value = jnp.where(high, high_c, low_c)
                if f == g:
                    value = value + (stor[f, a] + 6.0 * cond[f])
                coef[f * NF + g, a] = value
        return carry

    lax.fori_loop(0, CA, build, 0)

    lane_c = lax.broadcasted_iota(jnp.int32, (8, CR), 1)
    row_c = lax.broadcasted_iota(jnp.int32, (CZ, CR), 0)

    def interior(it):
        def body(a, carry):
            for h in range(2):
                top = 8 + 8 * h
                held = [dirs[it, g, a + 1, top : top + 8, :] for g in range(NF)]
                for f in range(NF):
                    acc = coef[f * NF, a, 8 * h : 8 * h + 8, :] * held[0]
                    for g in range(1, NF):
                        acc = acc + coef[f * NF + g, a, 8 * h : 8 * h + 8, :] * held[g]
                    near = dirs[it, f, a, top : top + 8, :] + dirs[it, f, a + 2, top : top + 8, :]
                    near = near + dirs[it, f, a + 1, top - 1 : top + 7, :]
                    near = near + dirs[it, f, a + 1, top + 1 : top + 9, :]
                    near = near + jnp.where(lane_c == 0, 0.0, pltpu.roll(held[f], 1, 1))
                    near = near + jnp.where(lane_c == CR - 1, 0.0, pltpu.roll(held[f], CR - 1, 1))
                    r_out[f, a, 8 * h : 8 * h + 8, :] = (
                        r_out[f, a, 8 * h : 8 * h + 8, :] - acc + cond[f] * near)
            return carry

        lax.fori_loop(0, CA, body, 0)

    first = jnp.where(ax == 0, 0.0, 1.0)
    last = jnp.where(ax == N_AXIAL - 1, 0.0, 1.0)
    scalars = steps()

    def finish(it, a):
        gain = 1.0 / center_value if it == 0 else 1.0
        for f in range(NF):
            c = cond[f]
            r = r_out[f, a]
            if a == 0:
                r = r + (c * first * gain) * halo_a[it, 0, f]
            if a == CA - 1:
                r = r + (c * last * gain) * halo_a[it, 1, f]
            r = r + c * (
                jnp.where(row_c == 0, halo_z[it, 0, f, a], 0.0)
                + jnp.where(row_c == CZ - 1, halo_z[it, 1, f, a], 0.0))
            r_out[f, a] = r
            if it + 1 < ITERS:
                alpha, beta = scalars[it]
                old = dirs[it, f, a + 1, 8:24, :]
                new = alpha * old + beta * r
                dirs[it + 1, f, a + 1, 8:24, :] = new
                pack_z[it + 1, 0, f, a] = new[0:1, :]
                pack_z[it + 1, 1, f, a] = new[CZ - 1 : CZ, :]
                if it == ITERS - 2:
                    x_out[f, a] = dirs[0, f, a + 1, 8:24, :] + old + new

    def wait_halos(it):
        for copy in halos[it]:
            copy.wait_recv()

    def advance(it):
        finish(it, 0)
        finish(it, CA - 1)
        nxt = send_axial(
            it + 1, dirs.at[it + 1, :, 1, 8:24, :], dirs.at[it + 1, :, CA, 8:24, :])
        finish(it, 1)
        finish(it, 2)
        halos.append(nxt + send_azim(it + 1))

    interior(0)
    wait_halos(0)
    advance(0)

    for copy in q_a:
        copy.wait_recv()
    ask_b[xy_pos] = ask_a[:, xy_pos]
    q_b = []
    for k in range(1, XY):
        q, dev = xy_peer(k)
        copy = pltpu.make_async_remote_copy(
            ask_a.at[:, q], ask_b.at[xy_pos], qb_send.at[k], qb_recv.at[k],
            device_id={"axial": dev}, device_id_type=MESH)
        copy.start()
        q_b.append(copy)

    radp[...] = jnp.zeros((RAD, RAD), jnp.float32)
    radp[0:PSLOT, :] = rad[...].astype(jnp.float32)
    interior(1)
    for copy in q_b:
        copy.wait_recv()

    panels = radp[...].astype(jnp.bfloat16)
    lane_r = lax.broadcasted_iota(jnp.int32, (ZN, ROWS, RAD), 2)
    sub_r = lax.broadcasted_iota(jnp.int32, (ZN, ROWS, RAD), 1)
    for q in range(XY):
        wanted = jnp.broadcast_to(ask_b[q], (ZN, ROWS, RAD))
        column = jnp.sum(
            jnp.where(lane_r == sub_r, wanted, 0), axis=2, keepdims=True)
        hot = ((lane_r == column) & (sub_r < CAP)).astype(jnp.float32)
        got = jnp.dot(
            hot.reshape(ZN * ROWS, RAD).astype(jnp.bfloat16), panels,
            preferred_element_type=jnp.float32)
        rows_out[q] = got.reshape(ZN, ROWS, RAD).astype(jnp.bfloat16)
    rows_a[xy_pos] = rows_out[xy_pos]
    p_a = []
    for k in range(1, XY):
        q, dev = xy_peer(k)
        copy = pltpu.make_async_remote_copy(
            rows_out.at[q], rows_a.at[xy_pos], pa_send.at[k], pa_recv.at[k],
            device_id={"axial": dev}, device_id_type=MESH)
        copy.start()
        p_a.append(copy)

    wait_halos(1)
    advance(1)

    for copy in p_a:
        copy.wait_recv()
    rows_b[z_pos] = rows_a[:, z_pos]
    p_b = []
    for k in range(1, ZN):
        z, dev = z_peer(k)
        copy = pltpu.make_async_remote_copy(
            rows_a.at[:, z], rows_b.at[z_pos], pb_send.at[k], pb_recv.at[k],
            device_id={"axial": dev}, device_id_type=MESH)
        copy.start()
        p_b.append(copy)

    interior(2)
    wait_halos(2)
    for a in range(CA):
        finish(2, a)

    for copy in p_b:
        copy.wait_recv()
    table = rows_b[...].astype(jnp.float32).reshape(N_AXIAL * ROWS, RAD).astype(jnp.bfloat16)
    columns = jnp.transpose(tcol[...])
    lane_t = lax.broadcasted_iota(jnp.int32, (RAD, N_AXIAL * ROWS), 1).astype(jnp.float32)
    picked, kinds = [], []
    for k in range(VIS):
        pick = (lane_t == columns[:, k : k + 1]).astype(jnp.float32).astype(jnp.bfloat16)
        picked.append(jnp.dot(pick, table, preferred_element_type=jnp.float32))
        kinds.append(columns[:, 8 + k : 9 + k])
    incoming = jnp.zeros((RAD, RAD), jnp.float32)
    for b in range(NB):
        grouped = jnp.zeros((RAD, RAD), jnp.float32)
        for k in range(VIS):
            grouped = grouped + jnp.where(kinds[k] == float(b), picked[k], 0.0)
        major = grouped.astype(jnp.bfloat16)
        minor = (grouped - major.astype(jnp.float32)).astype(jnp.bfloat16)
        for part in (major, minor):
            incoming = incoming + lax.dot_general(
                part, view[b], (((1,), (1,)), ((), ())),
                preferred_element_type=jnp.float32)
    wall = x_out[0, :, :, CR - RAD :].reshape(CA * CZ, RAD)[:, RAD - 1 :]
    wall = jnp.concatenate([wall, wall], axis=0)
    slots = lax.broadcasted_iota(jnp.int32, (PSLOT, RAD), 0)
    result = emission[...] * wall[0:PSLOT] + reflect[...] * incoming[0:PSLOT]
    rad_out[...] = jnp.where(slots < live_count, result, 0.0)

    for group in halos + [q_a, q_b, p_a, p_b]:
        for copy in group:
            copy.wait_send()


def body(
    source, storage, materials, conductance, mixing, counts, vis_owner, vis_slot, vis_block,
    radiosity_old, view_blocks, emission, reflect,
):
    vm = pl.BlockSpec(memory_space=pltpu.VMEM)
    sm = pl.BlockSpec(memory_space=pltpu.SMEM)
    anywhere = pl.BlockSpec(memory_space=pl.ANY)
    dma = pltpu.SemaphoreType.DMA
    f32, i32, b16 = jnp.float32, jnp.int32, jnp.bfloat16
    x, r, rad = pl.pallas_call(
        kernel,
        out_shape=(
            jax.ShapeDtypeStruct((NF, CA, CZ, CR), f32),
            jax.ShapeDtypeStruct((NF, CA, CZ, CR), f32),
            jax.ShapeDtypeStruct((PSLOT, RAD), f32),
        ),
        in_specs=[anywhere, anywhere, anywhere, sm, sm, sm, vm, vm, vm, vm, vm, vm, vm],
        out_specs=(vm, vm, vm),
        scratch_shapes=[
            pltpu.VMEM((ITERS, NF, CA + 2, CZ + 16, CR), f32),
            pltpu.VMEM((NF * NF, CA, CZ, CR), f32),
            pltpu.VMEM((NF, CA, CZ, CR), f32),
            pltpu.VMEM((CA, CZ, CR), i32),
            pltpu.VMEM((ITERS, 2, NF, CZ, CR), f32),
            pltpu.VMEM((ITERS, 2, NF, CA, 1, CR), f32),
            pltpu.VMEM((ITERS, 2, NF, CA, 1, CR), f32),
            pltpu.VMEM((ZN, XY, 1, RAD), i32),
            pltpu.VMEM((ZN, XY, 1, RAD), i32),
            pltpu.VMEM((XY, ZN, 1, RAD), i32),
            pltpu.VMEM((XY, ZN, ROWS, RAD), b16),
            pltpu.VMEM((XY, ZN, ROWS, RAD), b16),
            pltpu.VMEM((ZN, XY, ROWS, RAD), b16),
            pltpu.VMEM((RAD, RAD), f32),
            pltpu.VMEM((24, RAD), i32),
            pltpu.VMEM((RAD, RAD), f32),
            dma((3,)),
            dma((ITERS, 2)), dma((ITERS, 2)), dma((ITERS, 2)), dma((ITERS, 2)),
            dma((ZN,)), dma((ZN,)), dma((XY,)), dma((XY,)),
            dma((XY,)), dma((XY,)), dma((ZN,)), dma((ZN,)),
        ],
        compiler_params=pltpu.CompilerParams(
            collective_id=0, has_side_effects=True, vmem_limit_bytes=56 * 1024 * 1024),
    )(
        source, storage, materials, conductance, mixing, counts,
        vis_owner[0, 0].T, vis_slot[0, 0].T, vis_block[0, 0].T,
        radiosity_old[0, 0], view_blocks, emission[0, 0], reflect[0, 0],
    )
    return x, r, rad[None, None]


def solution(mesh):
    return jax.shard_map(
        body,
        mesh=mesh,
        in_specs=(
            P(None, "axial", "azim", None),
            P(None, "axial", "azim", None),
            P("axial", "azim", None),
            P(),
            P(),
            P("axial", "azim"),
            P("axial", "azim", None, None),
            P("axial", "azim", None, None),
            P("axial", "azim", None, None),
            P("axial", "azim", None, None),
            P(),
            P("axial", "azim", None, None),
            P("axial", "azim", None, None),
        ),
        out_specs=(
            P(None, "axial", "azim", None),
            P(None, "axial", "azim", None),
            P("axial", "azim", None, None),
        ),
        check_vma=False,
    )
```

```python
import functools

import jax
import jax.numpy as jnp
from jax import lax
from jax.experimental import pallas as pl
from jax.experimental.pallas import tpu as pltpu
from jax.sharding import PartitionSpec as P

NF = 12
MATS = 4
VIS = 4
NB = 8
ITERS = 3
CA = 4
CZ = 16
CR = 256
PSLOT = 120
RAD = 128
N_AXIAL = 96
N_AZIM = 8
XN = 4
ZN = 12
YN = 2
XY = XN * YN
CAP = 5
ROWS = 8
NCH = 3
FC = NF // NCH
BOUND = 24.0
LEVELS = 32760.0

center_value = 14.2
half_width = 13.8
MESH = pl.DeviceIdType.MESH


def steps():
    spread = center_value / half_width
    ratio = 1.0 / spread
    out = []
    for _ in range(ITERS - 1):
        after = 1.0 / (2.0 * spread - ratio)
        out.append((after * ratio, 2.0 * after / half_width))
        ratio = after
    return out


def kernel(
    source, storage, materials, cond, mixing, counts, owner, slot, block, rad, view,
    emission, reflect,
    x_out, r_out, rad_out,
    dirs, coef, stor, mats, face_in, face_out, side_in, side_out,
    fscale_in, fscale_out, sscale_in, sscale_out, side_f, pack_f,
    ask, ask_a, ask_b, rows_out, rows_a, rows_b, radp, idx, tcol,
    load_sem, fa_send, fa_recv, fs_send, fs_recv, sa_send, sa_recv, ss_send, ss_recv,
    qa_send, qa_recv, qb_send, qb_recv, pa_send, pa_recv, pb_send, pb_recv,
):
    ax = lax.axis_index("axial")
    az = lax.axis_index("azim")
    y_pos = ax % YN
    xz = ax // YN
    z_pos = xz % ZN
    x_pos = xz // ZN
    xy_pos = x_pos * YN + y_pos

    def z_peer(k):
        z = (z_pos + k) % ZN
        return z, (x_pos * ZN + z) * YN + y_pos

    def xy_peer(k):
        q = (xy_pos + k) % XY
        return q, ((q // YN) * ZN + z_pos) * YN + q % YN

    before = (ax + N_AXIAL - 1) % N_AXIAL
    after = (ax + 1) % N_AXIAL
    left = (az + N_AZIM - 1) % N_AZIM
    right = (az + 1) % N_AZIM

    loads = [
        pltpu.make_async_copy(source, r_out, load_sem.at[0]),
        pltpu.make_async_copy(materials, mats, load_sem.at[1]),
        pltpu.make_async_copy(storage, stor, load_sem.at[2]),
    ]
    for copy in loads:
        copy.start()

    barrier = pltpu.get_barrier_semaphore()
    for dev in (before, after):
        pl.semaphore_signal(barrier, inc=1, device_id={"axial": dev}, device_id_type=MESH)
    for dev in (left, right):
        pl.semaphore_signal(barrier, inc=1, device_id={"azim": dev}, device_id_type=MESH)
    for k in range(1, ZN):
        pl.semaphore_signal(barrier, inc=1, device_id={"axial": z_peer(k)[1]}, device_id_type=MESH)
    for k in range(1, XY):
        pl.semaphore_signal(barrier, inc=1, device_id={"axial": xy_peer(k)[1]}, device_id_type=MESH)

    def zero_rims(a, carry):
        for it in range(ITERS):
            for f in range(NF):
                dirs[it, f, a, 0:8, :] = jnp.zeros((8, CR), jnp.float32)
                dirs[it, f, a, 24:32, :] = jnp.zeros((8, CR), jnp.float32)
        return carry

    lax.fori_loop(1, CA + 1, zero_rims, 0)
    for it in range(ITERS):
        for f in range(NF):
            dirs[it, f, 0, 8:24, :] = jnp.zeros((CZ, CR), jnp.float32)
            dirs[it, f, CA + 1, 8:24, :] = jnp.zeros((CZ, CR), jnp.float32)

    pl.semaphore_wait(barrier, 4 + (ZN - 1) + (XY - 1))

    def fixed(values, inverse):
        return jnp.round(values * inverse).astype(jnp.int32).astype(jnp.int16)

    def wide(coded):
        return coded.astype(jnp.int32).astype(jnp.float32)

    halos = {}

    def send_pair(it, c, key, out, into, send, recv, axis, low, high):
        pair = []
        for side, dev in ((0, low), (1, high)):
            copy = pltpu.make_async_remote_copy(
                out(side), into(1 - side), send.at[it, c, side], recv.at[it, c, 1 - side],
                device_id={axis: dev}, device_id_type=MESH)
            copy.start()
            pair.append(copy)
        halos[key, it, c] = pair

    def send_sides(it, c):
        if it > 0:
            send_pair(
                it, c, "ss", lambda s: sscale_out.at[it, s, c], lambda s: sscale_in.at[it, s, c],
                ss_send, ss_recv, "azim", left, right)
        send_pair(
            it, c, "sa", lambda s: side_out.at[it, s, c], lambda s: side_in.at[it, s, c],
            sa_send, sa_recv, "azim", left, right)

    def send_faces(it, c):
        group = pl.ds(c * FC, FC)
        if it > 0:
            send_pair(
                it, c, "fs", lambda s: fscale_out.at[it, s, c], lambda s: fscale_in.at[it, s, c],
                fs_send, fs_recv, "axial", before, after)
        send_pair(
            it, c, "fa", lambda s: face_out.at[it, s, group], lambda s: face_in.at[it, s, group],
            fa_send, fa_recv, "axial", before, after)

    loads[0].wait()
    for c in range(NCH):
        for fl in range(FC):
            f = c * FC + fl
            for a in range(CA):
                value = r_out[f, a]
                dirs[0, f, a + 1, 8:24, :] = value * (1.0 / center_value)
                row = fl * CA + a
                pack_f[0, row : row + 1, :] = value[0:1, :]
                pack_f[1, row : row + 1, :] = value[CZ - 1 : CZ, :]
                if a in (0, CA - 1):
                    face_out[0, a // (CA - 1), f] = fixed(value, LEVELS / BOUND)
        for side in range(2):
            side_out[0, side, c] = fixed(pack_f[side], LEVELS / BOUND)
        send_sides(0, c)
        send_faces(0, c)

    live_count = counts[0, 0]
    lane = lax.broadcasted_iota(jnp.int32, (1, RAD), 1)
    live = lane < live_count
    idx[...] = jnp.zeros((24, RAD), jnp.int32)
    idx[0:VIS, 0:PSLOT] = owner[...]
    idx[8 : 8 + VIS, 0:PSLOT] = slot[...]
    idx[16 : 16 + VIS, 0:PSLOT] = block[...]
    sub96 = lax.broadcasted_iota(jnp.int32, (N_AXIAL, RAD), 0)
    lane96 = lax.broadcasted_iota(jnp.int32, (N_AXIAL, RAD), 1)
    upper = (
        lax.broadcasted_iota(jnp.int32, (RAD, RAD), 0)
        < lax.broadcasted_iota(jnp.int32, (RAD, RAD), 1)
    ).astype(jnp.float32).astype(jnp.bfloat16)
    ones = jnp.ones((RAD, RAD), jnp.bfloat16)
    past = jnp.zeros((N_AXIAL, RAD), jnp.float32)
    hits, ranks = [], []
    tcol[...] = jnp.zeros((RAD, RAD), jnp.float32)
    for k in range(VIS):
        own = idx[k : k + 1, :]
        y_of = own % YN
        t = own // YN
        x_of = (
            (t >= ZN).astype(jnp.int32)
            + (t >= 2 * ZN).astype(jnp.int32)
            + (t >= 3 * ZN).astype(jnp.int32)
        )
        place = (t - ZN * x_of) * XY + x_of * YN + y_of
        place = jnp.where(live, place, -1)
        hit = (sub96 == place).astype(jnp.float32)
        hit_b = hit.astype(jnp.bfloat16)
        rank = jnp.dot(hit_b, upper, preferred_element_type=jnp.float32)
        if k > 0:
            rank = rank + jnp.dot(
                past.astype(jnp.bfloat16), ones, preferred_element_type=jnp.float32)
        past = past + hit
        hits.append(hit)
        ranks.append(rank)
        mine = jnp.sum(hit * rank, axis=0, keepdims=True)
        tcol[k : k + 1, :] = place.astype(jnp.float32) * ROWS + mine
        tcol[8 + k : 9 + k, :] = idx[16 + k : 17 + k, :].astype(jnp.float32)
    asked = jnp.full((N_AXIAL, RAD), -1, jnp.int32)
    for r in range(CAP):
        total = jnp.zeros((N_AXIAL, RAD), jnp.float32)
        for k in range(VIS):
            wanted = (idx[8 + k : 9 + k, :] + 1).astype(jnp.float32)
            total = total + jnp.where(ranks[k] == float(r), hits[k] * wanted, 0.0)
        value = jnp.sum(total, axis=1, keepdims=True).astype(jnp.int32) - 1
        asked = jnp.where(lane96 == r, value, asked)
    ask[...] = asked.reshape(ZN, XY, 1, RAD)
    ask_a[z_pos] = ask[z_pos]
    q_a = []
    for k in range(1, ZN):
        z, dev = z_peer(k)
        copy = pltpu.make_async_remote_copy(
            ask.at[z], ask_a.at[z_pos], qa_send.at[k], qa_recv.at[k],
            device_id={"axial": dev}, device_id_type=MESH)
        copy.start()
        q_a.append(copy)

    for copy in loads[1:]:
        copy.wait()

    def build(a, carry):
        kind = mats[a]
        odd = (kind % 2) == 1
        high = kind >= 2
        for f in range(NF):
            for g in range(NF):
                low_c = jnp.where(odd, mixing[f, 1, g], mixing[f, 0, g])
                high_c = jnp.where(odd, mixing[f, 3, g], mixing[f, 2, g])
                value = jnp.where(high, high_c, low_c)
                if f == g:
                    value = value + (stor[f, a] + 6.0 * cond[f])
                coef[f * NF + g, a] = value
        return carry

    lax.fori_loop(0, CA, build, 0)

    lane_c = lax.broadcasted_iota(jnp.int32, (8, CR), 1)
    row_c = lax.broadcasted_iota(jnp.int32, (CZ, CR), 0)

    def interior(it):
        def body(a, carry):
            for h in range(2):
                top = 8 + 8 * h
                held = [dirs[it, g, a + 1, top : top + 8, :] for g in range(NF)]
                for f in range(NF):
                    acc = coef[f * NF, a, 8 * h : 8 * h + 8, :] * held[0]
                    for g in range(1, NF):
                        acc = acc + coef[f * NF + g, a, 8 * h : 8 * h + 8, :] * held[g]
                    near = dirs[it, f, a, top : top + 8, :] + dirs[it, f, a + 2, top : top + 8, :]
                    near = near + dirs[it, f, a + 1, top - 1 : top + 7, :]
                    near = near + dirs[it, f, a + 1, top + 1 : top + 9, :]
                    near = near + jnp.where(lane_c == 0, 0.0, pltpu.roll(held[f], 1, 1))
                    near = near + jnp.where(lane_c == CR - 1, 0.0, pltpu.roll(held[f], CR - 1, 1))
                    r_out[f, a, 8 * h : 8 * h + 8, :] = (
                        r_out[f, a, 8 * h : 8 * h + 8, :] - acc + cond[f] * near)
            return carry

        lax.fori_loop(0, CA, body, 0)

    first = jnp.where(ax == 0, 0.0, 1.0)
    last = jnp.where(ax == N_AXIAL - 1, 0.0, 1.0)
    scalars = steps()

    unit = BOUND / LEVELS / center_value

    def arrived(key, it, c, side):
        halos[key, it, c][1 - side].wait_recv()

    def finish(it, c):
        for side in range(2):
            if it > 0:
                arrived("ss", it, c, side)
            arrived("sa", it, c, side)
            scale = sscale_in[it, side, c] if it > 0 else unit
            side_f[side] = wide(side_in[it, side, c]) * scale
        tops = {}
        for a in (1, 2, 0, 3):
            end = a // (CA - 1)
            if a in (0, CA - 1):
                if it > 0:
                    arrived("fs", it, c, end)
                arrived("fa", it, c, end)
                scale = fscale_in[it, end, c] if it > 0 else unit
                scale = scale * (first if a == 0 else last)
            top = jnp.zeros((CZ, CR), jnp.float32)
            for fl in range(FC):
                f = c * FC + fl
                row = fl * CA + a
                add = (
                    jnp.where(row_c == 0, side_f[0, row : row + 1, :], 0.0)
                    + jnp.where(row_c == CZ - 1, side_f[1, row : row + 1, :], 0.0))
                if a in (0, CA - 1):
                    add = add + wide(face_in[it, end, f]) * scale
                r = r_out[f, a] + cond[f] * add
                r_out[f, a] = r
                if it + 1 < ITERS:
                    alpha, beta = scalars[it]
                    old = dirs[it, f, a + 1, 8:24, :]
                    new = alpha * old + beta * r
                    dirs[it + 1, f, a + 1, 8:24, :] = new
                    pack_f[0, row : row + 1, :] = new[0:1, :]
                    pack_f[1, row : row + 1, :] = new[CZ - 1 : CZ, :]
                    if a in (0, CA - 1):
                        top = jnp.maximum(top, jnp.abs(new))
                    if it == ITERS - 2:
                        x_out[f, a] = dirs[0, f, a + 1, 8:24, :] + old + new
            tops[a] = top
        if it + 1 == ITERS:
            return
        for side in range(2):
            rows = pack_f[side]
            high = jnp.maximum(jnp.max(jnp.abs(rows), axis=0, keepdims=True), 1e-30)
            sscale_out[it + 1, side, c] = high * (1.0 / LEVELS)
            side_out[it + 1, side, c] = fixed(rows, LEVELS / high)
        send_sides(it + 1, c)
        for end in range(2):
            a = end * (CA - 1)
            high = jnp.maximum(jnp.max(tops[a], axis=0, keepdims=True), 1e-30)
            fscale_out[it + 1, end, c] = high * (1.0 / LEVELS)
            inverse = LEVELS / high
            for f in range(c * FC, c * FC + FC):
                face_out[it + 1, end, f] = fixed(dirs[it + 1, f, a + 1, 8:24, :], inverse)
        send_faces(it + 1, c)

    radp[...] = jnp.zeros((RAD, RAD), jnp.float32)
    radp[0:PSLOT, :] = rad[...].astype(jnp.float32)
    for copy in q_a:
        copy.wait_recv()
    ask_b[xy_pos] = ask_a[:, xy_pos]
    q_b = []
    for k in range(1, XY):
        q, dev = xy_peer(k)
        copy = pltpu.make_async_remote_copy(
            ask_a.at[:, q], ask_b.at[xy_pos], qb_send.at[k], qb_recv.at[k],
            device_id={"axial": dev}, device_id_type=MESH)
        copy.start()
        q_b.append(copy)

    interior(0)
    for copy in q_b:
        copy.wait_recv()

    panels = radp[...].astype(jnp.bfloat16)
    lane_r = lax.broadcasted_iota(jnp.int32, (ZN, ROWS, RAD), 2)
    sub_r = lax.broadcasted_iota(jnp.int32, (ZN, ROWS, RAD), 1)
    for q in range(XY):
        wanted = jnp.broadcast_to(ask_b[q], (ZN, ROWS, RAD))
        column = jnp.sum(
            jnp.where(lane_r == sub_r, wanted, 0), axis=2, keepdims=True)
        hot = ((lane_r == column) & (sub_r < CAP)).astype(jnp.float32)
        got = jnp.dot(
            hot.reshape(ZN * ROWS, RAD).astype(jnp.bfloat16), panels,
            preferred_element_type=jnp.float32)
        rows_out[q] = got.reshape(ZN, ROWS, RAD).astype(jnp.bfloat16)
    rows_a[xy_pos] = rows_out[xy_pos]
    p_a = []
    for k in range(1, XY):
        q, dev = xy_peer(k)
        copy = pltpu.make_async_remote_copy(
            rows_out.at[q], rows_a.at[xy_pos], pa_send.at[k], pa_recv.at[k],
            device_id={"axial": dev}, device_id_type=MESH)
        copy.start()
        p_a.append(copy)

    for c in range(NCH):
        finish(0, c)
    interior(1)

    for copy in p_a:
        copy.wait_recv()
    rows_b[z_pos] = rows_a[:, z_pos]
    p_b = []
    for k in range(1, ZN):
        z, dev = z_peer(k)
        copy = pltpu.make_async_remote_copy(
            rows_a.at[:, z], rows_b.at[z_pos], pb_send.at[k], pb_recv.at[k],
            device_id={"axial": dev}, device_id_type=MESH)
        copy.start()
        p_b.append(copy)

    for c in range(NCH):
        finish(1, c)
    interior(2)

    for copy in p_b:
        copy.wait_recv()
    table = rows_b[...].astype(jnp.float32).reshape(N_AXIAL * ROWS, RAD).astype(jnp.bfloat16)
    columns = jnp.transpose(tcol[...])
    lane_t = lax.broadcasted_iota(jnp.int32, (RAD, N_AXIAL * ROWS), 1).astype(jnp.float32)
    picked, kinds = [], []
    for k in range(VIS):
        pick = (lane_t == columns[:, k : k + 1]).astype(jnp.float32).astype(jnp.bfloat16)
        picked.append(jnp.dot(pick, table, preferred_element_type=jnp.float32))
        kinds.append(columns[:, 8 + k : 9 + k])
    incoming = jnp.zeros((RAD, RAD), jnp.float32)
    for b in range(NB):
        grouped = jnp.zeros((RAD, RAD), jnp.float32)
        for k in range(VIS):
            grouped = grouped + jnp.where(kinds[k] == float(b), picked[k], 0.0)
        major = grouped.astype(jnp.bfloat16)
        minor = (grouped - major.astype(jnp.float32)).astype(jnp.bfloat16)
        for part in (major, minor):
            incoming = incoming + lax.dot_general(
                part, view[b], (((1,), (1,)), ((), ())),
                preferred_element_type=jnp.float32)
    wall = x_out[0, :, :, CR - RAD :].reshape(CA * CZ, RAD)[:, RAD - 1 :]
    wall = jnp.concatenate([wall, wall], axis=0)
    slots = lax.broadcasted_iota(jnp.int32, (PSLOT, RAD), 0)
    result = emission[...] * wall[0:PSLOT] + reflect[...] * incoming[0:PSLOT]
    rad_out[...] = jnp.where(slots < live_count, result, 0.0)

    for c in range(NCH):
        finish(2, c)

    for group in list(halos.values()) + [q_a, q_b, p_a, p_b]:
        for copy in group:
            copy.wait_send()


def body(
    source, storage, materials, conductance, mixing, counts, vis_owner, vis_slot, vis_block,
    radiosity_old, view_blocks, emission, reflect,
):
    vm = pl.BlockSpec(memory_space=pltpu.VMEM)
    sm = pl.BlockSpec(memory_space=pltpu.SMEM)
    anywhere = pl.BlockSpec(memory_space=pl.ANY)
    dma = pltpu.SemaphoreType.DMA
    f32, i32, i16, b16 = jnp.float32, jnp.int32, jnp.int16, jnp.bfloat16
    x, r, rad = pl.pallas_call(
        kernel,
        out_shape=(
            pltpu.VMEM((NF, CA, CZ, CR), f32),
            pltpu.VMEM((NF, CA, CZ, CR), f32),
            pltpu.VMEM((PSLOT, RAD), f32),
        ),
        in_specs=[anywhere, anywhere, anywhere, sm, sm, sm, vm, vm, vm, vm, vm, vm, vm],
        out_specs=(vm, vm, vm),
        scratch_shapes=[
            pltpu.VMEM((ITERS, NF, CA + 2, CZ + 16, CR), f32),
            pltpu.VMEM((NF * NF, CA, CZ, CR), f32),
            pltpu.VMEM((NF, CA, CZ, CR), f32),
            pltpu.VMEM((CA, CZ, CR), i32),
            pltpu.VMEM((ITERS, 2, NF, CZ, CR), i16),
            pltpu.VMEM((ITERS, 2, NF, CZ, CR), i16),
            pltpu.VMEM((ITERS, 2, NCH, FC * CA, CR), i16),
            pltpu.VMEM((ITERS, 2, NCH, FC * CA, CR), i16),
            pltpu.VMEM((ITERS, 2, NCH, 1, CR), f32),
            pltpu.VMEM((ITERS, 2, NCH, 1, CR), f32),
            pltpu.VMEM((ITERS, 2, NCH, 1, CR), f32),
            pltpu.VMEM((ITERS, 2, NCH, 1, CR), f32),
            pltpu.VMEM((2, FC * CA, CR), f32),
            pltpu.VMEM((2, FC * CA, CR), f32),
            pltpu.VMEM((ZN, XY, 1, RAD), i32),
            pltpu.VMEM((ZN, XY, 1, RAD), i32),
            pltpu.VMEM((XY, ZN, 1, RAD), i32),
            pltpu.VMEM((XY, ZN, ROWS, RAD), b16),
            pltpu.VMEM((XY, ZN, ROWS, RAD), b16),
            pltpu.VMEM((ZN, XY, ROWS, RAD), b16),
            pltpu.VMEM((RAD, RAD), f32),
            pltpu.VMEM((24, RAD), i32),
            pltpu.VMEM((RAD, RAD), f32),
            dma((3,)),
            *[dma((ITERS, NCH, 2)) for _ in range(8)],
            dma((ZN,)), dma((ZN,)), dma((XY,)), dma((XY,)),
            dma((XY,)), dma((XY,)), dma((ZN,)), dma((ZN,)),
        ],
        compiler_params=pltpu.CompilerParams(
            collective_id=0, has_side_effects=True, vmem_limit_bytes=56 * 1024 * 1024),
    )(
        source, storage, materials, conductance, jnp.transpose(mixing, (1, 0, 2)), counts,
        vis_owner[0, 0].T, vis_slot[0, 0].T, vis_block[0, 0].T,
        radiosity_old[0, 0], view_blocks, emission[0, 0], reflect[0, 0],
    )
    return x, r, rad[None, None]


def solution(mesh):
    return jax.shard_map(
        body,
        mesh=mesh,
        in_specs=(
            P(None, "axial", "azim", None),
            P(None, "axial", "azim", None),
            P("axial", "azim", None),
            P(),
            P(),
            P("axial", "azim"),
            P("axial", "azim", None, None),
            P("axial", "azim", None, None),
            P("axial", "azim", None, None),
            P("axial", "azim", None, None),
            P(),
            P("axial", "azim", None, None),
            P("axial", "azim", None, None),
        ),
        out_specs=(
            P(None, "axial", "azim", None),
            P(None, "axial", "azim", None),
            P("axial", "azim", None, None),
        ),
        check_vma=False,
    )
```

```python
import functools

import jax
import jax.numpy as jnp
from jax import lax
from jax.experimental import pallas as pl
from jax.experimental.pallas import tpu as pltpu
from jax.sharding import PartitionSpec as P

NF = 12
MATS = 4
VIS = 4
NB = 8
ITERS = 3
CA = 4
CZ = 16
CR = 256
PSLOT = 120
RAD = 128
N_AXIAL = 96
N_AZIM = 8
XN = 4
ZN = 12
YN = 2
XY = XN * YN
CAP = 5
ROWS = 8
NCH = 3
FC = NF // NCH
BOUND = 24.0
LEVELS = 32760.0

center_value = 14.2
half_width = 13.8
MESH = pl.DeviceIdType.MESH


def steps():
    spread = center_value / half_width
    ratio = 1.0 / spread
    out = []
    for _ in range(ITERS - 1):
        after = 1.0 / (2.0 * spread - ratio)
        out.append((after * ratio, 2.0 * after / half_width))
        ratio = after
    return out


def kernel(
    source, storage, materials, cond, mixing, counts, owner_h, slot_h, block_h, rad_h, view_h,
    emission_h, reflect_h,
    x_out, r_out, rad_out,
    dirs, coef, stor, mats, face_in, face_out, side_in, side_out,
    fscale_in, fscale_out, sscale_in, sscale_out, side_f, pack_f,
    ask, ask_a, ask_b, rows_out, rows_a, rows_b, radp, idx, tcol,
    owner, slot, block, rad, view, emission, reflect, ask_t,
    load_sem, fa_send, fa_recv, fs_send, fs_recv, sa_send, sa_recv, ss_send, ss_recv,
    qa_send, qa_recv, qb_send, qb_recv, pa_send, pa_recv, pb_send, pb_recv,
):
    ax = lax.axis_index("axial")
    az = lax.axis_index("azim")
    y_pos = ax % YN
    xz = ax // YN
    z_pos = xz % ZN
    x_pos = xz // ZN
    xy_pos = x_pos * YN + y_pos

    def z_peer(k):
        z = (z_pos + k) % ZN
        return z, (x_pos * ZN + z) * YN + y_pos

    def xy_peer(k):
        q = (xy_pos + k) % XY
        return q, ((q // YN) * ZN + z_pos) * YN + q % YN

    before = (ax + N_AXIAL - 1) % N_AXIAL
    after = (ax + 1) % N_AXIAL
    left = (az + N_AZIM - 1) % N_AZIM
    right = (az + 1) % N_AZIM

    loads = [
        pltpu.make_async_copy(source, r_out, load_sem.at[0]),
        pltpu.make_async_copy(materials, mats, load_sem.at[1]),
        pltpu.make_async_copy(storage, stor, load_sem.at[2]),
    ]
    index_loads = [
        pltpu.make_async_copy(owner_h, owner, load_sem.at[3]),
        pltpu.make_async_copy(slot_h, slot, load_sem.at[4]),
        pltpu.make_async_copy(block_h, block, load_sem.at[5]),
    ]
    panel_loads = [
        pltpu.make_async_copy(rad_h, rad, load_sem.at[6]),
        pltpu.make_async_copy(view_h, view, load_sem.at[7]),
        pltpu.make_async_copy(emission_h, emission, load_sem.at[8]),
        pltpu.make_async_copy(reflect_h, reflect, load_sem.at[9]),
    ]
    for copy in loads[:1] + index_loads + loads[1:] + panel_loads:
        copy.start()

    barrier = pltpu.get_barrier_semaphore()
    for dev in (before, after):
        pl.semaphore_signal(barrier, inc=1, device_id={"axial": dev}, device_id_type=MESH)
    for dev in (left, right):
        pl.semaphore_signal(barrier, inc=1, device_id={"azim": dev}, device_id_type=MESH)
    for k in range(1, ZN):
        pl.semaphore_signal(barrier, inc=1, device_id={"axial": z_peer(k)[1]}, device_id_type=MESH)
    for k in range(1, XY):
        pl.semaphore_signal(barrier, inc=1, device_id={"axial": xy_peer(k)[1]}, device_id_type=MESH)

    def zero_rims(a, carry):
        for it in range(ITERS):
            for f in range(NF):
                dirs[it, f, a, 0:8, :] = jnp.zeros((8, CR), jnp.float32)
                dirs[it, f, a, 24:32, :] = jnp.zeros((8, CR), jnp.float32)
        return carry

    lax.fori_loop(1, CA + 1, zero_rims, 0)
    for it in range(ITERS):
        for f in range(NF):
            dirs[it, f, 0, 8:24, :] = jnp.zeros((CZ, CR), jnp.float32)
            dirs[it, f, CA + 1, 8:24, :] = jnp.zeros((CZ, CR), jnp.float32)

    pl.semaphore_wait(barrier, 4 + (ZN - 1) + (XY - 1))

    def fixed(values, inverse):
        return jnp.round(values * inverse).astype(jnp.int32).astype(jnp.int16)

    def wide(coded):
        return coded.astype(jnp.int32).astype(jnp.float32)

    halos = {}

    def send_pair(it, c, key, out, into, send, recv, axis, low, high):
        pair = []
        for side, dev in ((0, low), (1, high)):
            copy = pltpu.make_async_remote_copy(
                out(side), into(1 - side), send.at[it, c, side], recv.at[it, c, 1 - side],
                device_id={axis: dev}, device_id_type=MESH)
            copy.start()
            pair.append(copy)
        halos[key, it, c] = pair

    def send_sides(it, c):
        if it > 0:
            send_pair(
                it, c, "ss", lambda s: sscale_out.at[it, s, c], lambda s: sscale_in.at[it, s, c],
                ss_send, ss_recv, "azim", left, right)
        send_pair(
            it, c, "sa", lambda s: side_out.at[it, s, c], lambda s: side_in.at[it, s, c],
            sa_send, sa_recv, "azim", left, right)

    def send_faces(it, c):
        group = pl.ds(c * FC, FC)
        if it > 0:
            send_pair(
                it, c, "fs", lambda s: fscale_out.at[it, s, c], lambda s: fscale_in.at[it, s, c],
                fs_send, fs_recv, "axial", before, after)
        send_pair(
            it, c, "fa", lambda s: face_out.at[it, s, group], lambda s: face_in.at[it, s, group],
            fa_send, fa_recv, "axial", before, after)

    def begin(c):
        for fl in range(FC):
            f = c * FC + fl
            for a in range(CA):
                value = r_out[f, a]
                dirs[0, f, a + 1, 8:24, :] = value * (1.0 / center_value)
                row = fl * CA + a
                pack_f[0, row : row + 1, :] = value[0:1, :]
                pack_f[1, row : row + 1, :] = value[CZ - 1 : CZ, :]
                if a in (0, CA - 1):
                    face_out[0, a // (CA - 1), f] = fixed(value, LEVELS / BOUND)
        for side in range(2):
            side_out[0, side, c] = fixed(pack_f[side], LEVELS / BOUND)
        send_sides(0, c)
        send_faces(0, c)

    loads[0].wait()
    begin(0)
    for copy in index_loads:
        copy.wait()

    live_count = counts[0, 0]
    lane = lax.broadcasted_iota(jnp.int32, (1, RAD), 1)
    live = lane < live_count
    idx[...] = jnp.zeros((24, RAD), jnp.int32)
    idx[0:VIS, 0:PSLOT] = owner[...]
    idx[8 : 8 + VIS, 0:PSLOT] = slot[...]
    idx[16 : 16 + VIS, 0:PSLOT] = block[...]
    sub96 = lax.broadcasted_iota(jnp.int32, (N_AXIAL, RAD), 0)
    lane96 = lax.broadcasted_iota(jnp.int32, (N_AXIAL, RAD), 1)
    upper = (
        lax.broadcasted_iota(jnp.int32, (RAD, RAD), 0)
        < lax.broadcasted_iota(jnp.int32, (RAD, RAD), 1)
    ).astype(jnp.float32).astype(jnp.bfloat16)
    ones = jnp.ones((RAD, RAD), jnp.bfloat16)
    past = jnp.zeros((N_AXIAL, RAD), jnp.float32)
    hits, ranks = [], []
    tcol[...] = jnp.zeros((RAD, RAD), jnp.float32)
    for k in range(VIS):
        own = idx[k : k + 1, :]
        y_of = own % YN
        t = own // YN
        x_of = (
            (t >= ZN).astype(jnp.int32)
            + (t >= 2 * ZN).astype(jnp.int32)
            + (t >= 3 * ZN).astype(jnp.int32)
        )
        place = (t - ZN * x_of) * XY + x_of * YN + y_of
        place = jnp.where(live, place, -1)
        hit = (sub96 == place).astype(jnp.float32)
        hit_b = hit.astype(jnp.bfloat16)
        rank = jnp.dot(hit_b, upper, preferred_element_type=jnp.float32)
        if k > 0:
            rank = rank + jnp.dot(
                past.astype(jnp.bfloat16), ones, preferred_element_type=jnp.float32)
        past = past + hit
        hits.append(hit)
        ranks.append(rank)
        mine = jnp.sum(hit * rank, axis=0, keepdims=True)
        tcol[k : k + 1, :] = place.astype(jnp.float32) * ROWS + mine
        tcol[8 + k : 9 + k, :] = idx[16 + k : 17 + k, :].astype(jnp.float32)
    asked = jnp.full((N_AXIAL, RAD), -1, jnp.int32)
    for r in range(CAP):
        total = jnp.zeros((N_AXIAL, RAD), jnp.float32)
        for k in range(VIS):
            wanted = (idx[8 + k : 9 + k, :] + 1).astype(jnp.float32)
            total = total + jnp.where(ranks[k] == float(r), hits[k] * wanted, 0.0)
        value = jnp.sum(total, axis=1, keepdims=True).astype(jnp.int32) - 1
        asked = jnp.where(lane96 == r, value, asked)
    ask[...] = asked.reshape(ZN, XY, 1, RAD)
    ask_a[z_pos] = ask[z_pos]
    q_a = []
    for k in range(1, ZN):
        z, dev = z_peer(k)
        copy = pltpu.make_async_remote_copy(
            ask.at[z], ask_a.at[z_pos], qa_send.at[k], qa_recv.at[k],
            device_id={"axial": dev}, device_id_type=MESH)
        copy.start()
        q_a.append(copy)

    for c in range(1, NCH):
        begin(c)

    for copy in loads[1:]:
        copy.wait()

    def build(a, carry):
        kind = mats[a]
        odd = (kind % 2) == 1
        high = kind >= 2
        for f in range(NF):
            for g in range(NF):
                low_c = jnp.where(odd, mixing[f, 1, g], mixing[f, 0, g])
                high_c = jnp.where(odd, mixing[f, 3, g], mixing[f, 2, g])
                value = jnp.where(high, high_c, low_c)
                if f == g:
                    value = value + (stor[f, a] + 6.0 * cond[f])
                coef[f * NF + g, a] = value
        return carry

    lax.fori_loop(0, CA, build, 0)

    lane_c = lax.broadcasted_iota(jnp.int32, (8, CR), 1)
    row_c = lax.broadcasted_iota(jnp.int32, (CZ, CR), 0)

    def interior(it):
        def body(a, carry):
            for h in range(2):
                top = 8 + 8 * h
                held = [dirs[it, g, a + 1, top : top + 8, :] for g in range(NF)]
                for f in range(NF):
                    acc = coef[f * NF, a, 8 * h : 8 * h + 8, :] * held[0]
                    for g in range(1, NF):
                        acc = acc + coef[f * NF + g, a, 8 * h : 8 * h + 8, :] * held[g]
                    near = dirs[it, f, a, top : top + 8, :] + dirs[it, f, a + 2, top : top + 8, :]
                    near = near + dirs[it, f, a + 1, top - 1 : top + 7, :]
                    near = near + dirs[it, f, a + 1, top + 1 : top + 9, :]
                    near = near + jnp.where(lane_c == 0, 0.0, pltpu.roll(held[f], 1, 1))
                    near = near + jnp.where(lane_c == CR - 1, 0.0, pltpu.roll(held[f], CR - 1, 1))
                    r_out[f, a, 8 * h : 8 * h + 8, :] = (
                        r_out[f, a, 8 * h : 8 * h + 8, :] - acc + cond[f] * near)
            return carry

        lax.fori_loop(0, CA, body, 0)

    first = jnp.where(ax == 0, 0.0, 1.0)
    last = jnp.where(ax == N_AXIAL - 1, 0.0, 1.0)
    scalars = steps()

    unit = BOUND / LEVELS / center_value

    def arrived(key, it, c, side):
        halos[key, it, c][1 - side].wait_recv()

    def finish(it, c):
        for side in range(2):
            if it > 0:
                arrived("ss", it, c, side)
            arrived("sa", it, c, side)
            scale = sscale_in[it, side, c] if it > 0 else unit
            side_f[side] = wide(side_in[it, side, c]) * scale
        tops = {}
        for a in (1, 2, 0, 3):
            end = a // (CA - 1)
            if a in (0, CA - 1):
                if it > 0:
                    arrived("fs", it, c, end)
                arrived("fa", it, c, end)
                scale = fscale_in[it, end, c] if it > 0 else unit
                scale = scale * (first if a == 0 else last)
            top = jnp.zeros((CZ, CR), jnp.float32)
            for fl in range(FC):
                f = c * FC + fl
                row = fl * CA + a
                add = (
                    jnp.where(row_c == 0, side_f[0, row : row + 1, :], 0.0)
                    + jnp.where(row_c == CZ - 1, side_f[1, row : row + 1, :], 0.0))
                if a in (0, CA - 1):
                    add = add + wide(face_in[it, end, f]) * scale
                r = r_out[f, a] + cond[f] * add
                r_out[f, a] = r
                if it + 1 < ITERS:
                    alpha, beta = scalars[it]
                    old = dirs[it, f, a + 1, 8:24, :]
                    new = alpha * old + beta * r
                    dirs[it + 1, f, a + 1, 8:24, :] = new
                    pack_f[0, row : row + 1, :] = new[0:1, :]
                    pack_f[1, row : row + 1, :] = new[CZ - 1 : CZ, :]
                    if a in (0, CA - 1):
                        top = jnp.maximum(top, jnp.abs(new))
                    if it == ITERS - 2:
                        x_out[f, a] = dirs[0, f, a + 1, 8:24, :] + old + new
            tops[a] = top
        if it + 1 == ITERS:
            return
        for side in range(2):
            rows = pack_f[side]
            high = jnp.maximum(jnp.max(jnp.abs(rows), axis=0, keepdims=True), 1e-30)
            sscale_out[it + 1, side, c] = high * (1.0 / LEVELS)
            side_out[it + 1, side, c] = fixed(rows, LEVELS / high)
        send_sides(it + 1, c)
        for end in range(2):
            a = end * (CA - 1)
            high = jnp.maximum(jnp.max(tops[a], axis=0, keepdims=True), 1e-30)
            fscale_out[it + 1, end, c] = high * (1.0 / LEVELS)
            inverse = LEVELS / high
            for f in range(c * FC, c * FC + FC):
                face_out[it + 1, end, f] = fixed(dirs[it + 1, f, a + 1, 8:24, :], inverse)
        send_faces(it + 1, c)

    for copy in q_a:
        copy.wait_recv()
    for q in range(XY):
        ask_t[q] = ask_a[:, q]
    ask_b[xy_pos] = ask_t[xy_pos]
    q_b = []
    for k in range(1, XY):
        q, dev = xy_peer(k)
        copy = pltpu.make_async_remote_copy(
            ask_t.at[q], ask_b.at[xy_pos], qb_send.at[k], qb_recv.at[k],
            device_id={"axial": dev}, device_id_type=MESH)
        copy.start()
        q_b.append(copy)

    interior(0)
    finish(0, 0)
    for copy in panel_loads:
        copy.wait()
    radp[...] = jnp.zeros((RAD, RAD), jnp.float32)
    radp[0:PSLOT, :] = rad[...].astype(jnp.float32)
    for copy in q_b:
        copy.wait_recv()

    panels = radp[...].astype(jnp.bfloat16)
    lane_r = lax.broadcasted_iota(jnp.int32, (ZN, ROWS, RAD), 2)
    sub_r = lax.broadcasted_iota(jnp.int32, (ZN, ROWS, RAD), 1)
    for q in range(XY):
        wanted = jnp.broadcast_to(ask_b[q], (ZN, ROWS, RAD))
        column = jnp.sum(
            jnp.where(lane_r == sub_r, wanted, 0), axis=2, keepdims=True)
        hot = ((lane_r == column) & (sub_r < CAP)).astype(jnp.float32)
        got = jnp.dot(
            hot.reshape(ZN * ROWS, RAD).astype(jnp.bfloat16), panels,
            preferred_element_type=jnp.float32)
        rows_out[q] = got.reshape(ZN, ROWS, RAD).astype(jnp.bfloat16)
    rows_a[xy_pos] = rows_out[xy_pos]
    p_a = []
    for k in range(1, XY):
        q, dev = xy_peer(k)
        copy = pltpu.make_async_remote_copy(
            rows_out.at[q], rows_a.at[xy_pos], pa_send.at[k], pa_recv.at[k],
            device_id={"axial": dev}, device_id_type=MESH)
        copy.start()
        p_a.append(copy)

    for c in range(1, NCH):
        finish(0, c)
    interior(1)

    for copy in p_a:
        copy.wait_recv()
    rows_b[z_pos] = rows_a[:, z_pos]
    p_b = []
    for k in range(1, ZN):
        z, dev = z_peer(k)
        copy = pltpu.make_async_remote_copy(
            rows_a.at[:, z], rows_b.at[z_pos], pb_send.at[k], pb_recv.at[k],
            device_id={"axial": dev}, device_id_type=MESH)
        copy.start()
        p_b.append(copy)

    for c in range(NCH):
        finish(1, c)
    interior(2)

    for copy in p_b:
        copy.wait_recv()
    table = rows_b[...].astype(jnp.float32).reshape(N_AXIAL * ROWS, RAD).astype(jnp.bfloat16)
    columns = jnp.transpose(tcol[...])
    lane_t = lax.broadcasted_iota(jnp.int32, (RAD, N_AXIAL * ROWS), 1).astype(jnp.float32)
    picked, kinds = [], []
    for k in range(VIS):
        pick = (lane_t == columns[:, k : k + 1]).astype(jnp.float32).astype(jnp.bfloat16)
        picked.append(jnp.dot(pick, table, preferred_element_type=jnp.float32))
        kinds.append(columns[:, 8 + k : 9 + k])
    incoming = jnp.zeros((RAD, RAD), jnp.float32)
    for b in range(NB):
        grouped = jnp.zeros((RAD, RAD), jnp.float32)
        for k in range(VIS):
            grouped = grouped + jnp.where(kinds[k] == float(b), picked[k], 0.0)
        major = grouped.astype(jnp.bfloat16)
        minor = (grouped - major.astype(jnp.float32)).astype(jnp.bfloat16)
        for part in (major, minor):
            incoming = incoming + lax.dot_general(
                part, view[b], (((1,), (1,)), ((), ())),
                preferred_element_type=jnp.float32)
    wall = x_out[0, :, :, CR - RAD :].reshape(CA * CZ, RAD)[:, RAD - 1 :]
    wall = jnp.concatenate([wall, wall], axis=0)
    slots = lax.broadcasted_iota(jnp.int32, (PSLOT, RAD), 0)
    result = emission[...] * wall[0:PSLOT] + reflect[...] * incoming[0:PSLOT]
    rad_out[...] = jnp.where(slots < live_count, result, 0.0)

    for c in range(NCH):
        finish(2, c)

    for group in list(halos.values()) + [q_a, q_b, p_a, p_b]:
        for copy in group:
            copy.wait_send()


def deliver(x, r, rad, x_out, r_out, rad_out, sem):
    copies = [
        pltpu.make_async_copy(x, x_out, sem.at[0]),
        pltpu.make_async_copy(r, r_out, sem.at[1]),
        pltpu.make_async_copy(rad, rad_out, sem.at[2]),
    ]
    for copy in copies:
        copy.start()
    for copy in copies:
        copy.wait()


def body(
    source, storage, materials, conductance, mixing, counts, vis_owner, vis_slot, vis_block,
    radiosity_old, view_blocks, emission, reflect,
):
    vm = pl.BlockSpec(memory_space=pltpu.VMEM)
    sm = pl.BlockSpec(memory_space=pltpu.SMEM)
    anywhere = pl.BlockSpec(memory_space=pl.ANY)
    dma = pltpu.SemaphoreType.DMA
    f32, i32, i16, b16 = jnp.float32, jnp.int32, jnp.int16, jnp.bfloat16
    x, r, rad = pl.pallas_call(
        kernel,
        out_shape=(
            pltpu.VMEM((NF, CA, CZ, CR), f32),
            pltpu.VMEM((NF, CA, CZ, CR), f32),
            pltpu.VMEM((PSLOT, RAD), f32),
        ),
        in_specs=[anywhere, anywhere, anywhere, sm, sm, sm] + [anywhere] * 7,
        out_specs=(vm, vm, vm),
        scratch_shapes=[
            pltpu.VMEM((ITERS, NF, CA + 2, CZ + 16, CR), f32),
            pltpu.VMEM((NF * NF, CA, CZ, CR), f32),
            pltpu.VMEM((NF, CA, CZ, CR), f32),
            pltpu.VMEM((CA, CZ, CR), i32),
            pltpu.VMEM((ITERS, 2, NF, CZ, CR), i16),
            pltpu.VMEM((ITERS, 2, NF, CZ, CR), i16),
            pltpu.VMEM((ITERS, 2, NCH, FC * CA, CR), i16),
            pltpu.VMEM((ITERS, 2, NCH, FC * CA, CR), i16),
            pltpu.VMEM((ITERS, 2, NCH, 1, CR), f32),
            pltpu.VMEM((ITERS, 2, NCH, 1, CR), f32),
            pltpu.VMEM((ITERS, 2, NCH, 1, CR), f32),
            pltpu.VMEM((ITERS, 2, NCH, 1, CR), f32),
            pltpu.VMEM((2, FC * CA, CR), f32),
            pltpu.VMEM((2, FC * CA, CR), f32),
            pltpu.VMEM((ZN, XY, 1, RAD), i32),
            pltpu.VMEM((ZN, XY, 1, RAD), i32),
            pltpu.VMEM((XY, ZN, 1, RAD), i32),
            pltpu.VMEM((XY, ZN, ROWS, RAD), b16),
            pltpu.VMEM((XY, ZN, ROWS, RAD), b16),
            pltpu.VMEM((ZN, XY, ROWS, RAD), b16),
            pltpu.VMEM((RAD, RAD), f32),
            pltpu.VMEM((24, RAD), i32),
            pltpu.VMEM((RAD, RAD), f32),
            pltpu.VMEM((VIS, PSLOT), i32),
            pltpu.VMEM((VIS, PSLOT), i32),
            pltpu.VMEM((VIS, PSLOT), i32),
            pltpu.VMEM((PSLOT, RAD), b16),
            pltpu.VMEM((NB, RAD, RAD), b16),
            pltpu.VMEM((PSLOT, RAD), f32),
            pltpu.VMEM((PSLOT, RAD), f32),
            pltpu.VMEM((XY, ZN, 1, RAD), i32),
            dma((10,)),
            *[dma((ITERS, NCH, 2)) for _ in range(8)],
            dma((ZN,)), dma((ZN,)), dma((XY,)), dma((XY,)),
            dma((XY,)), dma((XY,)), dma((ZN,)), dma((ZN,)),
        ],
        compiler_params=pltpu.CompilerParams(
            collective_id=0, has_side_effects=True, vmem_limit_bytes=56 * 1024 * 1024),
    )(
        source, storage, materials, conductance, jnp.transpose(mixing, (1, 0, 2)), counts,
        vis_owner[0, 0].T, vis_slot[0, 0].T, vis_block[0, 0].T,
        radiosity_old[0, 0], view_blocks, emission[0, 0], reflect[0, 0],
    )
    x, r, rad = pl.pallas_call(
        deliver,
        out_shape=(
            jax.ShapeDtypeStruct((NF, CA, CZ, CR), f32),
            jax.ShapeDtypeStruct((NF, CA, CZ, CR), f32),
            jax.ShapeDtypeStruct((PSLOT, RAD), f32),
        ),
        in_specs=[vm, vm, vm],
        out_specs=(anywhere, anywhere, anywhere),
        scratch_shapes=[dma((3,))],
    )(*(pltpu.with_memory_space_constraint(part, pltpu.VMEM) for part in (x, r, rad)))
    return x, r, rad[None, None]


def solution(mesh):
    return jax.shard_map(
        body,
        mesh=mesh,
        in_specs=(
            P(None, "axial", "azim", None),
            P(None, "axial", "azim", None),
            P("axial", "azim", None),
            P(),
            P(),
            P("axial", "azim"),
            P("axial", "azim", None, None),
            P("axial", "azim", None, None),
            P("axial", "azim", None, None),
            P("axial", "azim", None, None),
            P(),
            P("axial", "azim", None, None),
            P("axial", "azim", None, None),
        ),
        out_specs=(
            P(None, "axial", "azim", None),
            P(None, "axial", "azim", None),
            P("axial", "azim", None, None),
        ),
        check_vma=False,
    )
```

```python
import functools

import jax
import jax.numpy as jnp
from jax import lax
from jax.experimental import pallas as pl
from jax.experimental.pallas import tpu as pltpu
from jax.sharding import PartitionSpec as P

NF = 12
MATS = 4
VIS = 4
NB = 8
ITERS = 3
CA = 4
CZ = 16
CR = 256
PSLOT = 120
RAD = 128
N_AXIAL = 96
N_AZIM = 8
XN = 4
ZN = 12
YN = 2
XY = XN * YN
CAP = 5
ROWS = 8
PAIRS = 3
NCH = 3
FC = NF // NCH
BOUND = 24.0
LEVELS = 32760.0

center_value = 14.2
half_width = 13.8
MESH = pl.DeviceIdType.MESH


def steps():
    spread = center_value / half_width
    ratio = 1.0 / spread
    out = []
    for _ in range(ITERS - 1):
        after = 1.0 / (2.0 * spread - ratio)
        out.append((after * ratio, 2.0 * after / half_width))
        ratio = after
    return out


def kernel(
    source, storage, materials, cond, mixing, counts, owner_h, slot_h, block_h, rad_h, view_h,
    emission_h, reflect_h,
    x_out, r_out, rad_out,
    dirs, coef, stor, mats, face_in, face_out, side_in, side_out,
    fscale_in, fscale_out, sscale_in, sscale_out, side_f, pack_f,
    ask, ask_a, ask_b, rows_out, rows_a, rows_b, radp, idx, tcol,
    owner, slot, block, rad, view, emission, reflect, ask_t,
    load_sem, fa_send, fa_recv, fs_send, fs_recv, sa_send, sa_recv, ss_send, ss_recv,
    qa_send, qa_recv, qb_send, qb_recv, pa_send, pa_recv, pb_send, pb_recv,
):
    ax = lax.axis_index("axial")
    az = lax.axis_index("azim")
    y_pos = ax % YN
    xz = ax // YN
    z_pos = xz % ZN
    x_pos = xz // ZN
    xy_pos = x_pos * YN + y_pos

    def z_peer(k):
        z = (z_pos + k) % ZN
        return z, (x_pos * ZN + z) * YN + y_pos

    def xy_peer(k):
        q = (xy_pos + k) % XY
        return q, ((q // YN) * ZN + z_pos) * YN + q % YN

    before = (ax + N_AXIAL - 1) % N_AXIAL
    after = (ax + 1) % N_AXIAL
    left = (az + N_AZIM - 1) % N_AZIM
    right = (az + 1) % N_AZIM

    loads = [
        pltpu.make_async_copy(source, r_out, load_sem.at[0]),
        pltpu.make_async_copy(materials, mats, load_sem.at[1]),
        pltpu.make_async_copy(storage, stor, load_sem.at[2]),
    ]
    index_loads = [
        pltpu.make_async_copy(owner_h, owner, load_sem.at[3]),
        pltpu.make_async_copy(slot_h, slot, load_sem.at[4]),
        pltpu.make_async_copy(block_h, block, load_sem.at[5]),
    ]
    panel_loads = [
        pltpu.make_async_copy(rad_h, rad, load_sem.at[6]),
        pltpu.make_async_copy(view_h, view, load_sem.at[7]),
        pltpu.make_async_copy(emission_h, emission, load_sem.at[8]),
        pltpu.make_async_copy(reflect_h, reflect, load_sem.at[9]),
    ]
    for copy in loads[:1] + index_loads + loads[1:] + panel_loads:
        copy.start()

    barrier = pltpu.get_barrier_semaphore()
    for dev in (before, after):
        pl.semaphore_signal(barrier, inc=1, device_id={"axial": dev}, device_id_type=MESH)
    for dev in (left, right):
        pl.semaphore_signal(barrier, inc=1, device_id={"azim": dev}, device_id_type=MESH)
    for k in range(1, ZN):
        pl.semaphore_signal(barrier, inc=1, device_id={"axial": z_peer(k)[1]}, device_id_type=MESH)
    for k in range(1, XY):
        pl.semaphore_signal(barrier, inc=1, device_id={"axial": xy_peer(k)[1]}, device_id_type=MESH)

    def zero_rims(a, carry):
        for it in range(ITERS):
            for f in range(NF):
                dirs[it, f, a, 0:8, :] = jnp.zeros((8, CR), jnp.float32)
                dirs[it, f, a, 24:32, :] = jnp.zeros((8, CR), jnp.float32)
        return carry

    lax.fori_loop(1, CA + 1, zero_rims, 0)
    for it in range(ITERS):
        for f in range(NF):
            dirs[it, f, 0, 8:24, :] = jnp.zeros((CZ, CR), jnp.float32)
            dirs[it, f, CA + 1, 8:24, :] = jnp.zeros((CZ, CR), jnp.float32)

    for copy in index_loads:
        copy.wait()

    live_count = counts[0, 0]
    lane = lax.broadcasted_iota(jnp.int32, (1, RAD), 1)
    live = lane < live_count
    idx[...] = jnp.zeros((24, RAD), jnp.int32)
    idx[0:VIS, 0:PSLOT] = owner[...]
    idx[8 : 8 + VIS, 0:PSLOT] = slot[...]
    idx[16 : 16 + VIS, 0:PSLOT] = block[...]
    sub96 = lax.broadcasted_iota(jnp.int32, (N_AXIAL, RAD), 0)
    lane96 = lax.broadcasted_iota(jnp.int32, (N_AXIAL, RAD), 1)
    upper = (
        lax.broadcasted_iota(jnp.int32, (RAD, RAD), 0)
        < lax.broadcasted_iota(jnp.int32, (RAD, RAD), 1)
    ).astype(jnp.float32).astype(jnp.bfloat16)
    ones = jnp.ones((RAD, RAD), jnp.bfloat16)
    past = jnp.zeros((N_AXIAL, RAD), jnp.float32)
    hits, ranks = [], []
    tcol[...] = jnp.zeros((RAD, RAD), jnp.float32)
    for k in range(VIS):
        own = idx[k : k + 1, :]
        y_of = own % YN
        t = own // YN
        x_of = (
            (t >= ZN).astype(jnp.int32)
            + (t >= 2 * ZN).astype(jnp.int32)
            + (t >= 3 * ZN).astype(jnp.int32)
        )
        z_of = t - ZN * x_of
        xy_of = x_of * YN + y_of
        place = z_of * XY + xy_of
        shelf = (xy_of * ZN + z_of) * 2 * PAIRS
        place = jnp.where(live, place, -1)
        hit = (sub96 == place).astype(jnp.float32)
        hit_b = hit.astype(jnp.bfloat16)
        rank = jnp.dot(hit_b, upper, preferred_element_type=jnp.float32)
        if k > 0:
            rank = rank + jnp.dot(
                past.astype(jnp.bfloat16), ones, preferred_element_type=jnp.float32)
        past = past + hit
        hits.append(hit)
        ranks.append(rank)
        mine = jnp.sum(hit * rank, axis=0, keepdims=True)
        tcol[k : k + 1, :] = jnp.where(live, shelf, -ROWS).astype(jnp.float32) + mine
        tcol[8 + k : 9 + k, :] = idx[16 + k : 17 + k, :].astype(jnp.float32)
    asked = jnp.full((N_AXIAL, RAD), -1, jnp.int32)
    for r in range(CAP):
        total = jnp.zeros((N_AXIAL, RAD), jnp.float32)
        for k in range(VIS):
            wanted = (idx[8 + k : 9 + k, :] + 1).astype(jnp.float32)
            total = total + jnp.where(ranks[k] == float(r), hits[k] * wanted, 0.0)
        value = jnp.sum(total, axis=1, keepdims=True).astype(jnp.int32) - 1
        asked = jnp.where(lane96 == r, value, asked)
    pl.semaphore_wait(barrier, 4 + (ZN - 1) + (XY - 1))

    def fixed(values, inverse):
        return jnp.round(values * inverse).astype(jnp.int32).astype(jnp.int16)

    def wide(coded):
        return coded.astype(jnp.int32).astype(jnp.float32)

    halos = {}

    def send_pair(it, c, key, out, into, send, recv, axis, low, high):
        pair = []
        for side, dev in ((0, low), (1, high)):
            copy = pltpu.make_async_remote_copy(
                out(side), into(1 - side), send.at[it, c, side], recv.at[it, c, 1 - side],
                device_id={axis: dev}, device_id_type=MESH)
            copy.start()
            pair.append(copy)
        halos[key, it, c] = pair

    def send_sides(it, c):
        if it > 0:
            send_pair(
                it, c, "ss", lambda s: sscale_out.at[it, s, c], lambda s: sscale_in.at[it, s, c],
                ss_send, ss_recv, "azim", left, right)
        send_pair(
            it, c, "sa", lambda s: side_out.at[it, s, c], lambda s: side_in.at[it, s, c],
            sa_send, sa_recv, "azim", left, right)

    def send_faces(it, c):
        group = pl.ds(c * FC, FC)
        if it > 0:
            send_pair(
                it, c, "fs", lambda s: fscale_out.at[it, s, c], lambda s: fscale_in.at[it, s, c],
                fs_send, fs_recv, "axial", before, after)
        send_pair(
            it, c, "fa", lambda s: face_out.at[it, s, group], lambda s: face_in.at[it, s, group],
            fa_send, fa_recv, "axial", before, after)

    def begin(c):
        for fl in range(FC):
            f = c * FC + fl
            for a in range(CA):
                value = r_out[f, a]
                dirs[0, f, a + 1, 8:24, :] = value * (1.0 / center_value)
                row = fl * CA + a
                pack_f[0, row : row + 1, :] = value[0:1, :]
                pack_f[1, row : row + 1, :] = value[CZ - 1 : CZ, :]
                if a in (0, CA - 1):
                    face_out[0, a // (CA - 1), f] = fixed(value, LEVELS / BOUND)
        for side in range(2):
            side_out[0, side, c] = fixed(pack_f[side], LEVELS / BOUND)
        send_sides(0, c)
        send_faces(0, c)

    ask[...] = asked.reshape(ZN, XY, 1, RAD)
    ask_a[z_pos] = ask[z_pos]
    q_a = []
    for k in range(1, ZN):
        z, dev = z_peer(k)
        copy = pltpu.make_async_remote_copy(
            ask.at[z], ask_a.at[z_pos], qa_send.at[k], qa_recv.at[k],
            device_id={"axial": dev}, device_id_type=MESH)
        copy.start()
        q_a.append(copy)

    loads[0].wait()
    begin(0)
    for c in range(1, NCH):
        begin(c)

    for copy in loads[1:]:
        copy.wait()

    def build(a, carry):
        kind = mats[a]
        odd = (kind % 2) == 1
        high = kind >= 2
        for f in range(NF):
            for g in range(NF):
                low_c = jnp.where(odd, mixing[f, 1, g], mixing[f, 0, g])
                high_c = jnp.where(odd, mixing[f, 3, g], mixing[f, 2, g])
                value = jnp.where(high, high_c, low_c)
                if f == g:
                    value = value + (stor[f, a] + 6.0 * cond[f])
                coef[f * NF + g, a] = value
        return carry

    lax.fori_loop(0, CA, build, 0)

    lane_c = lax.broadcasted_iota(jnp.int32, (8, CR), 1)
    row_c = lax.broadcasted_iota(jnp.int32, (CZ, CR), 0)

    def interior(it):
        def body(a, carry):
            for h in range(2):
                top = 8 + 8 * h
                held = [dirs[it, g, a + 1, top : top + 8, :] for g in range(NF)]
                for f in range(NF):
                    acc = coef[f * NF, a, 8 * h : 8 * h + 8, :] * held[0]
                    for g in range(1, NF):
                        acc = acc + coef[f * NF + g, a, 8 * h : 8 * h + 8, :] * held[g]
                    near = dirs[it, f, a, top : top + 8, :] + dirs[it, f, a + 2, top : top + 8, :]
                    near = near + dirs[it, f, a + 1, top - 1 : top + 7, :]
                    near = near + dirs[it, f, a + 1, top + 1 : top + 9, :]
                    near = near + jnp.where(lane_c == 0, 0.0, pltpu.roll(held[f], 1, 1))
                    near = near + jnp.where(lane_c == CR - 1, 0.0, pltpu.roll(held[f], CR - 1, 1))
                    r_out[f, a, 8 * h : 8 * h + 8, :] = (
                        r_out[f, a, 8 * h : 8 * h + 8, :] - acc + cond[f] * near)
            return carry

        lax.fori_loop(0, CA, body, 0)

    first = jnp.where(ax == 0, 0.0, 1.0)
    last = jnp.where(ax == N_AXIAL - 1, 0.0, 1.0)
    scalars = steps()

    unit = BOUND / LEVELS / center_value

    def arrived(key, it, c, side):
        halos[key, it, c][1 - side].wait_recv()

    def finish(it, c):
        for side in range(2):
            if it > 0:
                arrived("ss", it, c, side)
            arrived("sa", it, c, side)
            scale = sscale_in[it, side, c] if it > 0 else unit
            side_f[side] = wide(side_in[it, side, c]) * scale
        tops = {}
        for a in (1, 2, 0, 3):
            end = a // (CA - 1)
            if a in (0, CA - 1):
                if it > 0:
                    arrived("fs", it, c, end)
                arrived("fa", it, c, end)
                scale = fscale_in[it, end, c] if it > 0 else unit
                scale = scale * (first if a == 0 else last)
            top = jnp.zeros((CZ, CR), jnp.float32)
            for fl in range(FC):
                f = c * FC + fl
                row = fl * CA + a
                add = (
                    jnp.where(row_c == 0, side_f[0, row : row + 1, :], 0.0)
                    + jnp.where(row_c == CZ - 1, side_f[1, row : row + 1, :], 0.0))
                if a in (0, CA - 1):
                    add = add + wide(face_in[it, end, f]) * scale
                r = r_out[f, a] + cond[f] * add
                r_out[f, a] = r
                if it + 1 < ITERS:
                    alpha, beta = scalars[it]
                    old = dirs[it, f, a + 1, 8:24, :]
                    new = alpha * old + beta * r
                    dirs[it + 1, f, a + 1, 8:24, :] = new
                    pack_f[0, row : row + 1, :] = new[0:1, :]
                    pack_f[1, row : row + 1, :] = new[CZ - 1 : CZ, :]
                    if a in (0, CA - 1):
                        top = jnp.maximum(top, jnp.abs(new))
                    if it == ITERS - 2:
                        x_out[f, a] = dirs[0, f, a + 1, 8:24, :] + old + new
            tops[a] = top
        if it + 1 == ITERS:
            return
        for side in range(2):
            rows = pack_f[side]
            high = jnp.maximum(jnp.max(jnp.abs(rows), axis=0, keepdims=True), 1e-30)
            sscale_out[it + 1, side, c] = high * (1.0 / LEVELS)
            side_out[it + 1, side, c] = fixed(rows, LEVELS / high)
        send_sides(it + 1, c)
        for end in range(2):
            a = end * (CA - 1)
            high = jnp.maximum(jnp.max(tops[a], axis=0, keepdims=True), 1e-30)
            fscale_out[it + 1, end, c] = high * (1.0 / LEVELS)
            inverse = LEVELS / high
            for f in range(c * FC, c * FC + FC):
                face_out[it + 1, end, f] = fixed(dirs[it + 1, f, a + 1, 8:24, :], inverse)
        send_faces(it + 1, c)

    for copy in q_a:
        copy.wait_recv()
    for q in range(XY):
        ask_t[q] = ask_a[:, q]
    ask_b[xy_pos] = ask_t[xy_pos]
    q_b = []
    for k in range(1, XY):
        q, dev = xy_peer(k)
        copy = pltpu.make_async_remote_copy(
            ask_t.at[q], ask_b.at[xy_pos], qb_send.at[k], qb_recv.at[k],
            device_id={"axial": dev}, device_id_type=MESH)
        copy.start()
        q_b.append(copy)

    interior(0)
    for c in range(NCH):
        finish(0, c)
    for copy in panel_loads:
        copy.wait()
    radp[...] = jnp.zeros((RAD, RAD), jnp.float32)
    radp[0:PSLOT, :] = rad[...].astype(jnp.float32)
    for copy in q_b:
        copy.wait_recv()

    panels = radp[...].astype(jnp.bfloat16)
    lane_r = lax.broadcasted_iota(jnp.int32, (XY, ROWS, RAD), 2)
    sub_r = lax.broadcasted_iota(jnp.int32, (XY, ROWS, RAD), 1)
    for z in range(ZN):
        wanted = jnp.broadcast_to(ask_b[:, z], (XY, ROWS, RAD))
        column = jnp.sum(
            jnp.where(lane_r == sub_r, wanted, 0), axis=2, keepdims=True)
        hot = ((lane_r == column) & (sub_r < CAP)).astype(jnp.float32)
        got = jnp.dot(
            hot.reshape(XY * ROWS, RAD).astype(jnp.bfloat16), panels,
            preferred_element_type=jnp.float32)
        got = got.reshape(XY, ROWS, RAD)
        for pair in range(PAIRS):
            rows_out[z, :, pair] = got[:, 2 * pair : 2 * pair + 2, :].astype(jnp.bfloat16)
    rows_a[z_pos] = rows_out[z_pos]
    p_a = []
    for k in range(1, ZN):
        z, dev = z_peer(k)
        copy = pltpu.make_async_remote_copy(
            rows_out.at[z], rows_a.at[z_pos], pb_send.at[k], pb_recv.at[k],
            device_id={"axial": dev}, device_id_type=MESH)
        copy.start()
        p_a.append(copy)

    interior(1)
    for c in range(NCH):
        finish(1, c)
    for copy in p_a:
        copy.wait_recv()
    rows_b[xy_pos] = rows_a[:, xy_pos]
    p_b = []
    for k in range(1, XY):
        q, dev = xy_peer(k)
        copy = pltpu.make_async_remote_copy(
            rows_a.at[:, q], rows_b.at[xy_pos], pa_send.at[k], pa_recv.at[k],
            device_id={"axial": dev}, device_id_type=MESH)
        copy.start()
        p_b.append(copy)

    interior(2)
    early = [pair for (_, it, _), pair in halos.items() if it < ITERS - 1]
    for group in early + [q_a, q_b, p_a]:
        for copy in group:
            copy.wait_send()
    for c in range(NCH):
        finish(2, c)


    for copy in p_b:
        copy.wait_recv()
    table = rows_b[...].astype(jnp.float32).reshape(N_AXIAL * 2 * PAIRS, RAD).astype(jnp.bfloat16)
    columns = jnp.transpose(tcol[...])
    lane_t = lax.broadcasted_iota(jnp.int32, (RAD, N_AXIAL * 2 * PAIRS), 1).astype(jnp.float32)
    picked, kinds = [], []
    for k in range(VIS):
        pick = (lane_t == columns[:, k : k + 1]).astype(jnp.float32).astype(jnp.bfloat16)
        picked.append(jnp.dot(pick, table, preferred_element_type=jnp.float32))
        kinds.append(columns[:, 8 + k : 9 + k])
    incoming = jnp.zeros((RAD, RAD), jnp.float32)
    for b in range(NB):
        grouped = jnp.zeros((RAD, RAD), jnp.float32)
        for k in range(VIS):
            grouped = grouped + jnp.where(kinds[k] == float(b), picked[k], 0.0)
        major = grouped.astype(jnp.bfloat16)
        minor = (grouped - major.astype(jnp.float32)).astype(jnp.bfloat16)
        for part in (major, minor):
            incoming = incoming + lax.dot_general(
                part, view[b], (((1,), (1,)), ((), ())),
                preferred_element_type=jnp.float32)
    wall = x_out[0, :, :, CR - RAD :].reshape(CA * CZ, RAD)[:, RAD - 1 :]
    wall = jnp.concatenate([wall, wall], axis=0)
    slots = lax.broadcasted_iota(jnp.int32, (PSLOT, RAD), 0)
    result = emission[...] * wall[0:PSLOT] + reflect[...] * incoming[0:PSLOT]
    rad_out[...] = jnp.where(slots < live_count, result, 0.0)

    late = [pair for (_, it, _), pair in halos.items() if it == ITERS - 1]
    for group in late + [p_b]:
        for copy in group:
            copy.wait_send()


def deliver(x, r, rad, x_out, r_out, rad_out, sem):
    copies = [
        pltpu.make_async_copy(x, x_out, sem.at[0]),
        pltpu.make_async_copy(r, r_out, sem.at[1]),
        pltpu.make_async_copy(rad, rad_out, sem.at[2]),
    ]
    for copy in copies:
        copy.start()
    for copy in copies:
        copy.wait()


def body(
    source, storage, materials, conductance, mixing, counts, vis_owner, vis_slot, vis_block,
    radiosity_old, view_blocks, emission, reflect,
):
    vm = pl.BlockSpec(memory_space=pltpu.VMEM)
    sm = pl.BlockSpec(memory_space=pltpu.SMEM)
    anywhere = pl.BlockSpec(memory_space=pl.ANY)
    dma = pltpu.SemaphoreType.DMA
    f32, i32, i16, b16 = jnp.float32, jnp.int32, jnp.int16, jnp.bfloat16
    x, r, rad = pl.pallas_call(
        kernel,
        out_shape=(
            pltpu.VMEM((NF, CA, CZ, CR), f32),
            pltpu.VMEM((NF, CA, CZ, CR), f32),
            pltpu.VMEM((PSLOT, RAD), f32),
        ),
        in_specs=[anywhere, anywhere, anywhere, sm, sm, sm] + [anywhere] * 7,
        out_specs=(vm, vm, vm),
        scratch_shapes=[
            pltpu.VMEM((ITERS, NF, CA + 2, CZ + 16, CR), f32),
            pltpu.VMEM((NF * NF, CA, CZ, CR), f32),
            pltpu.VMEM((NF, CA, CZ, CR), f32),
            pltpu.VMEM((CA, CZ, CR), i32),
            pltpu.VMEM((ITERS, 2, NF, CZ, CR), i16),
            pltpu.VMEM((ITERS, 2, NF, CZ, CR), i16),
            pltpu.VMEM((ITERS, 2, NCH, FC * CA, CR), i16),
            pltpu.VMEM((ITERS, 2, NCH, FC * CA, CR), i16),
            pltpu.VMEM((ITERS, 2, NCH, 1, CR), f32),
            pltpu.VMEM((ITERS, 2, NCH, 1, CR), f32),
            pltpu.VMEM((ITERS, 2, NCH, 1, CR), f32),
            pltpu.VMEM((ITERS, 2, NCH, 1, CR), f32),
            pltpu.VMEM((2, FC * CA, CR), f32),
            pltpu.VMEM((2, FC * CA, CR), f32),
            pltpu.VMEM((ZN, XY, 1, RAD), i32),
            pltpu.VMEM((ZN, XY, 1, RAD), i32),
            pltpu.VMEM((XY, ZN, 1, RAD), i32),
            pltpu.VMEM((ZN, XY, PAIRS, 2, RAD), b16),
            pltpu.VMEM((ZN, XY, PAIRS, 2, RAD), b16),
            pltpu.VMEM((XY, ZN, PAIRS, 2, RAD), b16),
            pltpu.VMEM((RAD, RAD), f32),
            pltpu.VMEM((24, RAD), i32),
            pltpu.VMEM((RAD, RAD), f32),
            pltpu.VMEM((VIS, PSLOT), i32),
            pltpu.VMEM((VIS, PSLOT), i32),
            pltpu.VMEM((VIS, PSLOT), i32),
            pltpu.VMEM((PSLOT, RAD), b16),
            pltpu.VMEM((NB, RAD, RAD), b16),
            pltpu.VMEM((PSLOT, RAD), f32),
            pltpu.VMEM((PSLOT, RAD), f32),
            pltpu.VMEM((XY, ZN, 1, RAD), i32),
            dma((10,)),
            *[dma((ITERS, NCH, 2)) for _ in range(8)],
            dma((ZN,)), dma((ZN,)), dma((XY,)), dma((XY,)),
            dma((XY,)), dma((XY,)), dma((ZN,)), dma((ZN,)),
        ],
        compiler_params=pltpu.CompilerParams(
            collective_id=0, has_side_effects=True, vmem_limit_bytes=56 * 1024 * 1024),
    )(
        source, storage, materials, conductance, jnp.transpose(mixing, (1, 0, 2)), counts,
        vis_owner[0, 0].T, vis_slot[0, 0].T, vis_block[0, 0].T,
        radiosity_old[0, 0], view_blocks, emission[0, 0], reflect[0, 0],
    )
    x, r, rad = pl.pallas_call(
        deliver,
        out_shape=(
            jax.ShapeDtypeStruct((NF, CA, CZ, CR), f32),
            jax.ShapeDtypeStruct((NF, CA, CZ, CR), f32),
            jax.ShapeDtypeStruct((PSLOT, RAD), f32),
        ),
        in_specs=[vm, vm, vm],
        out_specs=(anywhere, anywhere, anywhere),
        scratch_shapes=[dma((3,))],
    )(*(pltpu.with_memory_space_constraint(part, pltpu.VMEM) for part in (x, r, rad)))
    return x, r, rad[None, None]


def solution(mesh):
    return jax.shard_map(
        body,
        mesh=mesh,
        in_specs=(
            P(None, "axial", "azim", None),
            P(None, "axial", "azim", None),
            P("axial", "azim", None),
            P(),
            P(),
            P("axial", "azim"),
            P("axial", "azim", None, None),
            P("axial", "azim", None, None),
            P("axial", "azim", None, None),
            P("axial", "azim", None, None),
            P(),
            P("axial", "azim", None, None),
            P("axial", "azim", None, None),
        ),
        out_specs=(
            P(None, "axial", "azim", None),
            P(None, "axial", "azim", None),
            P("axial", "azim", None, None),
        ),
        check_vma=False,
    )
```

```python
import functools

import jax
import jax.numpy as jnp
from jax import lax
from jax.experimental import pallas as pl
from jax.experimental.pallas import tpu as pltpu
from jax.sharding import PartitionSpec as P

NF = 12
MATS = 4
VIS = 4
NB = 8
ITERS = 3
CA = 4
CZ = 16
CR = 256
PSLOT = 120
RAD = 128
N_AXIAL = 96
N_AZIM = 8
XN = 4
ZN = 12
YN = 2
XY = XN * YN
CAP = 5
ROWS = 8
PAIRS = 3
NCH = 2
FC = NF // NCH
BOUND = 24.0
LEVELS = 32760.0

center_value = 14.2
half_width = 13.8
MESH = pl.DeviceIdType.MESH


def steps():
    spread = center_value / half_width
    ratio = 1.0 / spread
    out = []
    for _ in range(ITERS - 1):
        after = 1.0 / (2.0 * spread - ratio)
        out.append((after * ratio, 2.0 * after / half_width))
        ratio = after
    return out


def kernel(
    source, storage, materials, cond, mixing, counts, owner_h, slot_h, block_h, rad_h, view_h,
    emission_h, reflect_h,
    x_out, r_out, rad_out,
    dirs, coef, stor, mats, face_in, face_out, side_in, side_out,
    fscale_in, fscale_out, sscale_in, sscale_out, side_f, pack_f,
    ask, ask_a, ask_b, rows_out, rows_a, rows_b, radp, idx, tcol,
    owner, slot, block, rad, view, emission, reflect, ask_t,
    load_sem, fa_send, fa_recv, fs_send, fs_recv, sa_send, sa_recv, ss_send, ss_recv,
    qa_send, qa_recv, qb_send, qb_recv, pa_send, pa_recv, pb_send, pb_recv,
):
    ax = lax.axis_index("axial")
    az = lax.axis_index("azim")
    y_pos = ax % YN
    xz = ax // YN
    z_pos = xz % ZN
    x_pos = xz // ZN
    xy_pos = x_pos * YN + y_pos

    def z_peer(k):
        z = (z_pos + k) % ZN
        return z, (x_pos * ZN + z) * YN + y_pos

    def xy_peer(k):
        q = (xy_pos + k) % XY
        return q, ((q // YN) * ZN + z_pos) * YN + q % YN

    before = (ax + N_AXIAL - 1) % N_AXIAL
    after = (ax + 1) % N_AXIAL
    left = (az + N_AZIM - 1) % N_AZIM
    right = (az + 1) % N_AZIM

    loads = [
        pltpu.make_async_copy(source, r_out, load_sem.at[0]),
        pltpu.make_async_copy(materials, mats, load_sem.at[1]),
        pltpu.make_async_copy(storage, stor, load_sem.at[2]),
    ]
    index_loads = [
        pltpu.make_async_copy(owner_h, owner, load_sem.at[3]),
        pltpu.make_async_copy(slot_h, slot, load_sem.at[4]),
        pltpu.make_async_copy(block_h, block, load_sem.at[5]),
    ]
    panel_loads = [
        pltpu.make_async_copy(rad_h, rad, load_sem.at[6]),
        pltpu.make_async_copy(view_h, view, load_sem.at[7]),
        pltpu.make_async_copy(emission_h, emission, load_sem.at[8]),
        pltpu.make_async_copy(reflect_h, reflect, load_sem.at[9]),
    ]
    for copy in loads[:1] + index_loads + loads[1:] + panel_loads:
        copy.start()

    barrier = pltpu.get_barrier_semaphore()
    for dev in (before, after):
        pl.semaphore_signal(barrier, inc=1, device_id={"axial": dev}, device_id_type=MESH)
    for dev in (left, right):
        pl.semaphore_signal(barrier, inc=1, device_id={"azim": dev}, device_id_type=MESH)
    for k in range(1, ZN):
        pl.semaphore_signal(barrier, inc=1, device_id={"axial": z_peer(k)[1]}, device_id_type=MESH)
    for k in range(1, XY):
        pl.semaphore_signal(barrier, inc=1, device_id={"axial": xy_peer(k)[1]}, device_id_type=MESH)

    def zero_rims(a, carry):
        for it in range(ITERS):
            for f in range(NF):
                dirs[it, f, a, 0:8, :] = jnp.zeros((8, CR), jnp.float32)
                dirs[it, f, a, 24:32, :] = jnp.zeros((8, CR), jnp.float32)
        return carry

    lax.fori_loop(1, CA + 1, zero_rims, 0)
    for it in range(ITERS):
        for f in range(NF):
            dirs[it, f, 0, 8:24, :] = jnp.zeros((CZ, CR), jnp.float32)
            dirs[it, f, CA + 1, 8:24, :] = jnp.zeros((CZ, CR), jnp.float32)

    for copy in index_loads:
        copy.wait()

    live_count = counts[0, 0]
    lane = lax.broadcasted_iota(jnp.int32, (1, RAD), 1)
    live = lane < live_count
    idx[...] = jnp.zeros((24, RAD), jnp.int32)
    idx[0:VIS, 0:PSLOT] = owner[...]
    idx[8 : 8 + VIS, 0:PSLOT] = slot[...]
    idx[16 : 16 + VIS, 0:PSLOT] = block[...]
    sub96 = lax.broadcasted_iota(jnp.int32, (N_AXIAL, RAD), 0)
    lane96 = lax.broadcasted_iota(jnp.int32, (N_AXIAL, RAD), 1)
    upper = (
        lax.broadcasted_iota(jnp.int32, (RAD, RAD), 0)
        < lax.broadcasted_iota(jnp.int32, (RAD, RAD), 1)
    ).astype(jnp.float32).astype(jnp.bfloat16)
    ones = jnp.ones((RAD, RAD), jnp.bfloat16)
    past = jnp.zeros((N_AXIAL, RAD), jnp.float32)
    hits, ranks = [], []
    tcol[...] = jnp.zeros((RAD, RAD), jnp.float32)
    for k in range(VIS):
        own = idx[k : k + 1, :]
        y_of = own % YN
        t = own // YN
        x_of = (
            (t >= ZN).astype(jnp.int32)
            + (t >= 2 * ZN).astype(jnp.int32)
            + (t >= 3 * ZN).astype(jnp.int32)
        )
        z_of = t - ZN * x_of
        xy_of = x_of * YN + y_of
        place = z_of * XY + xy_of
        shelf = (xy_of * ZN + z_of) * 2 * PAIRS
        place = jnp.where(live, place, -1)
        hit = (sub96 == place).astype(jnp.float32)
        hit_b = hit.astype(jnp.bfloat16)
        rank = jnp.dot(hit_b, upper, preferred_element_type=jnp.float32)
        if k > 0:
            rank = rank + jnp.dot(
                past.astype(jnp.bfloat16), ones, preferred_element_type=jnp.float32)
        past = past + hit
        hits.append(hit)
        ranks.append(rank)
        mine = jnp.sum(hit * rank, axis=0, keepdims=True)
        tcol[k : k + 1, :] = jnp.where(live, shelf, -ROWS).astype(jnp.float32) + mine
        tcol[8 + k : 9 + k, :] = idx[16 + k : 17 + k, :].astype(jnp.float32)
    asked = jnp.full((N_AXIAL, RAD), -1, jnp.int32)
    for r in range(CAP):
        total = jnp.zeros((N_AXIAL, RAD), jnp.float32)
        for k in range(VIS):
            wanted = (idx[8 + k : 9 + k, :] + 1).astype(jnp.float32)
            total = total + jnp.where(ranks[k] == float(r), hits[k] * wanted, 0.0)
        value = jnp.sum(total, axis=1, keepdims=True).astype(jnp.int32) - 1
        asked = jnp.where(lane96 == r, value, asked)
    pl.semaphore_wait(barrier, 4 + (ZN - 1) + (XY - 1))

    def fixed(values, inverse):
        return jnp.round(values * inverse).astype(jnp.int32).astype(jnp.int16)

    def wide(coded):
        return coded.astype(jnp.int32).astype(jnp.float32)

    halos = {}

    def send_pair(it, c, key, out, into, send, recv, axis, low, high):
        pair = []
        for side, dev in ((0, low), (1, high)):
            copy = pltpu.make_async_remote_copy(
                out(side), into(1 - side), send.at[it, c, side], recv.at[it, c, 1 - side],
                device_id={axis: dev}, device_id_type=MESH)
            copy.start()
            pair.append(copy)
        halos[key, it, c] = pair

    def send_sides(it, c):
        if it > 0:
            send_pair(
                it, c, "ss", lambda s: sscale_out.at[it, s, c], lambda s: sscale_in.at[it, s, c],
                ss_send, ss_recv, "azim", left, right)
        send_pair(
            it, c, "sa", lambda s: side_out.at[it, s, c], lambda s: side_in.at[it, s, c],
            sa_send, sa_recv, "azim", left, right)

    def send_faces(it, c):
        group = pl.ds(c * FC, FC)
        if it > 0:
            send_pair(
                it, c, "fs", lambda s: fscale_out.at[it, s, c], lambda s: fscale_in.at[it, s, c],
                fs_send, fs_recv, "axial", before, after)
        send_pair(
            it, c, "fa", lambda s: face_out.at[it, s, group], lambda s: face_in.at[it, s, group],
            fa_send, fa_recv, "axial", before, after)

    def begin(c):
        for fl in range(FC):
            f = c * FC + fl
            for a in range(CA):
                value = r_out[f, a]
                dirs[0, f, a + 1, 8:24, :] = value * (1.0 / center_value)
                row = fl * CA + a
                pack_f[0, row : row + 1, :] = value[0:1, :]
                pack_f[1, row : row + 1, :] = value[CZ - 1 : CZ, :]
                if a in (0, CA - 1):
                    face_out[0, a // (CA - 1), f] = fixed(value, LEVELS / BOUND)
        for side in range(2):
            side_out[0, side, c] = fixed(pack_f[side], LEVELS / BOUND)
        send_sides(0, c)
        send_faces(0, c)

    ask[...] = asked.reshape(ZN, XY, 1, RAD)
    ask_a[z_pos] = ask[z_pos]
    q_a = []
    for k in range(1, ZN):
        z, dev = z_peer(k)
        copy = pltpu.make_async_remote_copy(
            ask.at[z], ask_a.at[z_pos], qa_send.at[k], qa_recv.at[k],
            device_id={"axial": dev}, device_id_type=MESH)
        copy.start()
        q_a.append(copy)

    loads[0].wait()
    begin(0)
    for c in range(1, NCH):
        begin(c)

    for copy in q_a:
        copy.wait_recv()
    for q in range(XY):
        ask_t[q] = ask_a[:, q]
    ask_b[xy_pos] = ask_t[xy_pos]
    q_b = []
    for k in range(1, XY):
        q, dev = xy_peer(k)
        copy = pltpu.make_async_remote_copy(
            ask_t.at[q], ask_b.at[xy_pos], qb_send.at[k], qb_recv.at[k],
            device_id={"axial": dev}, device_id_type=MESH)
        copy.start()
        q_b.append(copy)

    for copy in loads[1:]:
        copy.wait()

    def build(a, carry):
        kind = mats[a]
        odd = (kind % 2) == 1
        high = kind >= 2
        for f in range(NF):
            for g in range(NF):
                low_c = jnp.where(odd, mixing[f, 1, g], mixing[f, 0, g])
                high_c = jnp.where(odd, mixing[f, 3, g], mixing[f, 2, g])
                value = jnp.where(high, high_c, low_c)
                if f == g:
                    value = value + (stor[f, a] + 6.0 * cond[f])
                coef[f * NF + g, a] = value
        return carry

    lax.fori_loop(0, CA, build, 0)

    lane_c = lax.broadcasted_iota(jnp.int32, (8, CR), 1)
    row_c = lax.broadcasted_iota(jnp.int32, (CZ, CR), 0)

    def interior(it, fields):
        def body(a, carry):
            for h in range(2):
                top = 8 + 8 * h
                held = [dirs[it, g, a + 1, top : top + 8, :] for g in range(NF)]
                for f in fields:
                    acc = coef[f * NF, a, 8 * h : 8 * h + 8, :] * held[0]
                    for g in range(1, NF):
                        acc = acc + coef[f * NF + g, a, 8 * h : 8 * h + 8, :] * held[g]
                    near = dirs[it, f, a, top : top + 8, :] + dirs[it, f, a + 2, top : top + 8, :]
                    near = near + dirs[it, f, a + 1, top - 1 : top + 7, :]
                    near = near + dirs[it, f, a + 1, top + 1 : top + 9, :]
                    near = near + jnp.where(lane_c == 0, 0.0, pltpu.roll(held[f], 1, 1))
                    near = near + jnp.where(lane_c == CR - 1, 0.0, pltpu.roll(held[f], CR - 1, 1))
                    r_out[f, a, 8 * h : 8 * h + 8, :] = (
                        r_out[f, a, 8 * h : 8 * h + 8, :] - acc + cond[f] * near)
            return carry

        lax.fori_loop(0, CA, body, 0)

    first = jnp.where(ax == 0, 0.0, 1.0)
    last = jnp.where(ax == N_AXIAL - 1, 0.0, 1.0)
    scalars = steps()

    unit = BOUND / LEVELS / center_value

    def arrived(key, it, c, side):
        halos[key, it, c][1 - side].wait_recv()

    def finish(it, c):
        for side in range(2):
            if it > 0:
                arrived("ss", it, c, side)
            arrived("sa", it, c, side)
            scale = sscale_in[it, side, c] if it > 0 else unit
            side_f[side] = wide(side_in[it, side, c]) * scale
        tops = {}
        for a in (1, 2, 0, 3):
            end = a // (CA - 1)
            if a in (0, CA - 1):
                if it > 0:
                    arrived("fs", it, c, end)
                arrived("fa", it, c, end)
                scale = fscale_in[it, end, c] if it > 0 else unit
                scale = scale * (first if a == 0 else last)
            top = jnp.zeros((CZ, CR), jnp.float32)
            for fl in range(FC):
                f = c * FC + fl
                row = fl * CA + a
                add = (
                    jnp.where(row_c == 0, side_f[0, row : row + 1, :], 0.0)
                    + jnp.where(row_c == CZ - 1, side_f[1, row : row + 1, :], 0.0))
                if a in (0, CA - 1):
                    add = add + wide(face_in[it, end, f]) * scale
                r = r_out[f, a] + cond[f] * add
                r_out[f, a] = r
                if it + 1 < ITERS:
                    alpha, beta = scalars[it]
                    old = dirs[it, f, a + 1, 8:24, :]
                    new = alpha * old + beta * r
                    dirs[it + 1, f, a + 1, 8:24, :] = new
                    pack_f[0, row : row + 1, :] = new[0:1, :]
                    pack_f[1, row : row + 1, :] = new[CZ - 1 : CZ, :]
                    if a in (0, CA - 1):
                        top = jnp.maximum(top, jnp.abs(new))
                    if it == ITERS - 2:
                        x_out[f, a] = dirs[0, f, a + 1, 8:24, :] + old + new
            tops[a] = top
        if it + 1 == ITERS:
            return
        for side in range(2):
            rows = pack_f[side]
            high = jnp.maximum(jnp.max(jnp.abs(rows), axis=0, keepdims=True), 1e-30)
            sscale_out[it + 1, side, c] = high * (1.0 / LEVELS)
            side_out[it + 1, side, c] = fixed(rows, LEVELS / high)
        send_sides(it + 1, c)
        for end in range(2):
            a = end * (CA - 1)
            high = jnp.maximum(jnp.max(tops[a], axis=0, keepdims=True), 1e-30)
            fscale_out[it + 1, end, c] = high * (1.0 / LEVELS)
            inverse = LEVELS / high
            for f in range(c * FC, c * FC + FC):
                face_out[it + 1, end, f] = fixed(dirs[it + 1, f, a + 1, 8:24, :], inverse)
        send_faces(it + 1, c)

    interior(0, range(FC))
    for c in range(NCH):
        if c + 1 < NCH:
            interior(0, range((c + 1) * FC, (c + 2) * FC))
        finish(0, c)
    for copy in panel_loads:
        copy.wait()
    radp[...] = jnp.zeros((RAD, RAD), jnp.float32)
    radp[0:PSLOT, :] = rad[...].astype(jnp.float32)
    for copy in q_b:
        copy.wait_recv()

    panels = radp[...].astype(jnp.bfloat16)
    lane_r = lax.broadcasted_iota(jnp.int32, (XY, ROWS, RAD), 2)
    sub_r = lax.broadcasted_iota(jnp.int32, (XY, ROWS, RAD), 1)
    for z in range(ZN):
        wanted = jnp.broadcast_to(ask_b[:, z], (XY, ROWS, RAD))
        column = jnp.sum(
            jnp.where(lane_r == sub_r, wanted, 0), axis=2, keepdims=True)
        hot = ((lane_r == column) & (sub_r < CAP)).astype(jnp.float32)
        got = jnp.dot(
            hot.reshape(XY * ROWS, RAD).astype(jnp.bfloat16), panels,
            preferred_element_type=jnp.float32)
        got = got.reshape(XY, ROWS, RAD)
        for pair in range(PAIRS):
            rows_out[z, :, pair] = got[:, 2 * pair : 2 * pair + 2, :].astype(jnp.bfloat16)
    rows_a[z_pos] = rows_out[z_pos]
    p_a = []
    for k in range(1, ZN):
        z, dev = z_peer(k)
        copy = pltpu.make_async_remote_copy(
            rows_out.at[z], rows_a.at[z_pos], pb_send.at[k], pb_recv.at[k],
            device_id={"axial": dev}, device_id_type=MESH)
        copy.start()
        p_a.append(copy)

    interior(1, range(FC))
    for c in range(NCH):
        if c + 1 < NCH:
            interior(1, range((c + 1) * FC, (c + 2) * FC))
        finish(1, c)
    for copy in p_a:
        copy.wait_recv()
    rows_b[xy_pos] = rows_a[:, xy_pos]
    p_b = []
    for k in range(1, XY):
        q, dev = xy_peer(k)
        copy = pltpu.make_async_remote_copy(
            rows_a.at[:, q], rows_b.at[xy_pos], pa_send.at[k], pa_recv.at[k],
            device_id={"axial": dev}, device_id_type=MESH)
        copy.start()
        p_b.append(copy)

    interior(2, range(NF))
    early = [pair for (_, it, _), pair in halos.items() if it < ITERS - 1]
    for group in early + [q_a, q_b, p_a]:
        for copy in group:
            copy.wait_send()
    for c in range(NCH):
        finish(2, c)


    for copy in p_b:
        copy.wait_recv()
    table = rows_b[...].astype(jnp.float32).reshape(N_AXIAL * 2 * PAIRS, RAD).astype(jnp.bfloat16)
    columns = jnp.transpose(tcol[...])
    lane_t = lax.broadcasted_iota(jnp.int32, (RAD, N_AXIAL * 2 * PAIRS), 1).astype(jnp.float32)
    picked, kinds = [], []
    for k in range(VIS):
        pick = (lane_t == columns[:, k : k + 1]).astype(jnp.float32).astype(jnp.bfloat16)
        picked.append(jnp.dot(pick, table, preferred_element_type=jnp.float32))
        kinds.append(columns[:, 8 + k : 9 + k])
    incoming = jnp.zeros((RAD, RAD), jnp.float32)
    for b in range(NB):
        grouped = jnp.zeros((RAD, RAD), jnp.float32)
        for k in range(VIS):
            grouped = grouped + jnp.where(kinds[k] == float(b), picked[k], 0.0)
        major = grouped.astype(jnp.bfloat16)
        minor = (grouped - major.astype(jnp.float32)).astype(jnp.bfloat16)
        for part in (major, minor):
            incoming = incoming + lax.dot_general(
                part, view[b], (((1,), (1,)), ((), ())),
                preferred_element_type=jnp.float32)
    wall = x_out[0, :, :, CR - RAD :].reshape(CA * CZ, RAD)[:, RAD - 1 :]
    wall = jnp.concatenate([wall, wall], axis=0)
    slots = lax.broadcasted_iota(jnp.int32, (PSLOT, RAD), 0)
    result = emission[...] * wall[0:PSLOT] + reflect[...] * incoming[0:PSLOT]
    rad_out[...] = jnp.where(slots < live_count, result, 0.0)

    late = [pair for (_, it, _), pair in halos.items() if it == ITERS - 1]
    for group in late + [p_b]:
        for copy in group:
            copy.wait_send()


def deliver(x, r, rad, x_out, r_out, rad_out, sem):
    copies = [
        pltpu.make_async_copy(x, x_out, sem.at[0]),
        pltpu.make_async_copy(r, r_out, sem.at[1]),
        pltpu.make_async_copy(rad, rad_out, sem.at[2]),
    ]
    for copy in copies:
        copy.start()
    for copy in copies:
        copy.wait()


def body(
    source, storage, materials, conductance, mixing, counts, vis_owner, vis_slot, vis_block,
    radiosity_old, view_blocks, emission, reflect,
):
    vm = pl.BlockSpec(memory_space=pltpu.VMEM)
    sm = pl.BlockSpec(memory_space=pltpu.SMEM)
    anywhere = pl.BlockSpec(memory_space=pl.ANY)
    dma = pltpu.SemaphoreType.DMA
    f32, i32, i16, b16 = jnp.float32, jnp.int32, jnp.int16, jnp.bfloat16
    x, r, rad = pl.pallas_call(
        kernel,
        out_shape=(
            pltpu.VMEM((NF, CA, CZ, CR), f32),
            pltpu.VMEM((NF, CA, CZ, CR), f32),
            pltpu.VMEM((PSLOT, RAD), f32),
        ),
        in_specs=[anywhere, anywhere, anywhere, sm, sm, sm] + [anywhere] * 7,
        out_specs=(vm, vm, vm),
        scratch_shapes=[
            pltpu.VMEM((ITERS, NF, CA + 2, CZ + 16, CR), f32),
            pltpu.VMEM((NF * NF, CA, CZ, CR), f32),
            pltpu.VMEM((NF, CA, CZ, CR), f32),
            pltpu.VMEM((CA, CZ, CR), i32),
            pltpu.VMEM((ITERS, 2, NF, CZ, CR), i16),
            pltpu.VMEM((ITERS, 2, NF, CZ, CR), i16),
            pltpu.VMEM((ITERS, 2, NCH, FC * CA, CR), i16),
            pltpu.VMEM((ITERS, 2, NCH, FC * CA, CR), i16),
            pltpu.VMEM((ITERS, 2, NCH, 1, CR), f32),
            pltpu.VMEM((ITERS, 2, NCH, 1, CR), f32),
            pltpu.VMEM((ITERS, 2, NCH, 1, CR), f32),
            pltpu.VMEM((ITERS, 2, NCH, 1, CR), f32),
            pltpu.VMEM((2, FC * CA, CR), f32),
            pltpu.VMEM((2, FC * CA, CR), f32),
            pltpu.VMEM((ZN, XY, 1, RAD), i32),
            pltpu.VMEM((ZN, XY, 1, RAD), i32),
            pltpu.VMEM((XY, ZN, 1, RAD), i32),
            pltpu.VMEM((ZN, XY, PAIRS, 2, RAD), b16),
            pltpu.VMEM((ZN, XY, PAIRS, 2, RAD), b16),
            pltpu.VMEM((XY, ZN, PAIRS, 2, RAD), b16),
            pltpu.VMEM((RAD, RAD), f32),
            pltpu.VMEM((24, RAD), i32),
            pltpu.VMEM((RAD, RAD), f32),
            pltpu.VMEM((VIS, PSLOT), i32),
            pltpu.VMEM((VIS, PSLOT), i32),
            pltpu.VMEM((VIS, PSLOT), i32),
            pltpu.VMEM((PSLOT, RAD), b16),
            pltpu.VMEM((NB, RAD, RAD), b16),
            pltpu.VMEM((PSLOT, RAD), f32),
            pltpu.VMEM((PSLOT, RAD), f32),
            pltpu.VMEM((XY, ZN, 1, RAD), i32),
            dma((10,)),
            *[dma((ITERS, NCH, 2)) for _ in range(8)],
            dma((ZN,)), dma((ZN,)), dma((XY,)), dma((XY,)),
            dma((XY,)), dma((XY,)), dma((ZN,)), dma((ZN,)),
        ],
        compiler_params=pltpu.CompilerParams(
            collective_id=0, has_side_effects=True, vmem_limit_bytes=56 * 1024 * 1024),
    )(
        source, storage, materials, conductance, jnp.transpose(mixing, (1, 0, 2)), counts,
        vis_owner[0, 0].T, vis_slot[0, 0].T, vis_block[0, 0].T,
        radiosity_old[0, 0], view_blocks, emission[0, 0], reflect[0, 0],
    )
    x, r, rad = pl.pallas_call(
        deliver,
        out_shape=(
            jax.ShapeDtypeStruct((NF, CA, CZ, CR), f32),
            jax.ShapeDtypeStruct((NF, CA, CZ, CR), f32),
            jax.ShapeDtypeStruct((PSLOT, RAD), f32),
        ),
        in_specs=[vm, vm, vm],
        out_specs=(anywhere, anywhere, anywhere),
        scratch_shapes=[dma((3,))],
    )(*(pltpu.with_memory_space_constraint(part, pltpu.VMEM) for part in (x, r, rad)))
    return x, r, rad[None, None]


def solution(mesh):
    return jax.shard_map(
        body,
        mesh=mesh,
        in_specs=(
            P(None, "axial", "azim", None),
            P(None, "axial", "azim", None),
            P("axial", "azim", None),
            P(),
            P(),
            P("axial", "azim"),
            P("axial", "azim", None, None),
            P("axial", "azim", None, None),
            P("axial", "azim", None, None),
            P("axial", "azim", None, None),
            P(),
            P("axial", "azim", None, None),
            P("axial", "azim", None, None),
        ),
        out_specs=(
            P(None, "axial", "azim", None),
            P(None, "axial", "azim", None),
            P("axial", "azim", None, None),
        ),
        check_vma=False,
    )
```
